128 devices in a mesh: dp: 16 (over y_lo, x, core), seq: 8 (over z, y_hi).
Axes of the slice: x: 4, y: 4 (y_hi: 2, y_lo: 2; y = y_hi * 2 + y_lo), z: 4, core: 2. Of those that a mesh axis runs over, the one named last changes fastest.
Arguments:
- queries: bfloat16 [16, 4096, 2048], P('dp', 'seq'), may hold values from -650 to 650
- keys_values: bfloat16 [16, 4096, 1024], P('dp', 'seq'), may hold values from -28 to 28
- doc_blocks: int32 [16, 32], P('dp'), may hold values from 0 to 7, never falling along the last dimension, each value on 1 to 16 neighbouring positions
- route_plan: int32 [8, 4], P('seq'), may hold values from 0 to 15, as said below
- out_weight: bfloat16 [2048, 4096], P('dp'), may hold values from -0.125 to 0.125
Outputs:
- layer_out: bfloat16 [16, 4096, 4096], P('dp', 'seq')
The draws below stay inside these ranges and needn't reach their ends.
Inputs may be any that keep to these rules, and one draw needn't show every extreme that they name: Within a row of route_plan the entries are distinct.
All inputs are finite; a program needn't handle non-finite values.
Results may differ from the reference program's by a relative error of at most 0.0053.
Values may be sent and summed in bfloat16 or wider, within the bound.
No kernel may reach another device: no remote copies, remote signals or barrier semaphores. Data moves between devices by JAX's collectives and lax.ppermute only.
A program may use at most 256 MiB of HBM per device.

```python
import math
import jax
import jax.numpy as jnp
import numpy as np
from jax import lax

D = 4096
HEADS = 16
KV_HEADS = 4
HEAD_DIM = 128
BLOCK = 128
SEQ_LEN = 4096
NB = 32
NBD = 4
N_DP = 16
N_SEQ = 8


def draw_pairs_base(key):
    base = jax.random.normal(jax.random.fold_in(key, 11), (N_DP, SEQ_LEN, KV_HEADS, 2, HEAD_DIM), jnp.float32)
    return base


def draw_keys_values(key, part):
    base = draw_pairs_base(key)
    return base.reshape(N_DP, SEQ_LEN, KV_HEADS * 2 * HEAD_DIM).astype(jnp.bfloat16)


def draw_queries(key, part):
    grouped = HEADS // KV_HEADS
    base = jax.random.normal(jax.random.fold_in(key, 21), (N_DP, SEQ_LEN, KV_HEADS, grouped, HEAD_DIM), jnp.float32)
    return base.reshape(N_DP, SEQ_LEN, HEADS * HEAD_DIM).astype(jnp.bfloat16)


def permute_one(sub_key):
    return jax.random.permutation(sub_key, N_DP)


def draw_route_plan(key, part):
    sub_keys = jax.random.split(jax.random.fold_in(key, 31), N_SEQ)
    orders = jax.vmap(permute_one)(sub_keys)
    return orders[:, :NBD].astype(jnp.int32)


def levels(stream_key, shape, cuts, least, top_value):
    loudness = 1.0
    for dim, blocks in cuts:
        draws = jax.random.uniform(jax.random.fold_in(jax.random.fold_in(stream_key, 6), dim), (blocks,), jnp.float32, least / len(cuts), top_value / len(cuts))
        loudness = loudness * jnp.repeat(jnp.exp(draws), shape[dim] // blocks).reshape((-1,) + (1,) * (len(shape) - 1 - dim))
    return loudness


def split_up(amount, total, reach, slope):
    portions = [(1 << 20) // math.isqrt(grade ** slope) + 1 for grade in range(2, amount + 1)]
    spare, given = total - reach - (amount - 1), [1] * (amount - 1)
    while spare > 0:
        movable = [i for i in range(amount - 1) if given[i] < reach]
        mass, budget = sum([portions[i] for i in movable]), spare
        for i in movable:
            more = min(reach - given[i], max(1, budget * portions[i] // mass), spare)
            given[i] = given[i] + more
            spare = spare - more
    return np.array([reach] + given)


def uneven_parts(own_key, count, total, most, slope):
    if count == 2:
        one = jax.random.randint(own_key, (), max(1, total - most), min(most, total - 1) + 1)
        return jnp.stack([one, total - one])
    sizes = jnp.asarray(split_up(count, total, most, slope), jnp.int32)
    twos = (count - 1) // 2
    source_of, taker = sizes[1:1 + 2 * twos:2], sizes[2:2 + 2 * twos:2]
    room = jnp.minimum(source_of - 1, most - taker)
    moved = jax.random.randint(jax.random.fold_in(own_key, 1), (twos,), 0, 1 << 20) % (room + 1)
    sizes = sizes.at[1:1 + 2 * twos:2].set(source_of - moved).at[2:2 + 2 * twos:2].set(taker + moved)
    return sizes[jax.random.permutation(jax.random.fold_in(own_key, 2), count)]


def gaussian(stream_key, dims, deviation, bound, cuts=(), kind=jnp.bfloat16):
    loudness = levels(stream_key, dims, cuts, -0.22, 0.18) if cuts else 1.0
    values = jax.random.normal(stream_key, dims, jnp.float32) * deviation * loudness
    return jnp.minimum(jnp.maximum(values, -bound), bound).astype(kind)


def setup_inputs(seed: int = 0) -> dict:
    streams_of = jax.random.split(jax.random.key(seed), 6)
    return {
        "queries": draw_queries(jax.random.fold_in(streams_of[5], 71), 0),
        "keys_values": draw_keys_values(jax.random.fold_in(streams_of[5], 71), 0),
        "doc_blocks": jax.vmap(lambda own: jnp.searchsorted(jnp.cumsum(uneven_parts(own, max(3, NB // 4), NB, max(2, NB // 2), 2)), jnp.arange(NB), side="right"))(jax.random.split(streams_of[2], N_DP)).reshape((N_DP, NB)).astype(jnp.int32),
        "route_plan": draw_route_plan(jax.random.fold_in(streams_of[5], 71), 0),
        "out_weight": gaussian(streams_of[4], (HEADS * HEAD_DIM, D), (HEADS * HEAD_DIM) ** -0.5, 0.125, ((0, 16),)),
    }


neg_fill = -1e+30

def attend_group(query_rows, pair_rows, doc_ids):
    seq_rows = query_rows.shape[0]
    grouped = HEADS // KV_HEADS
    query_view = query_rows.reshape(seq_rows, KV_HEADS, grouped, HEAD_DIM).astype(jnp.float32)
    pair_view = pair_rows.reshape(seq_rows, KV_HEADS, 2, HEAD_DIM).astype(jnp.float32)
    key_view = pair_view[:, :, 0]
    value_view = pair_view[:, :, 1]
    token_doc = jnp.repeat(doc_ids, BLOCK)
    tile_rows = min(512, seq_rows)
    key_pos = jnp.arange(seq_rows, dtype=jnp.int32)
    score_scale = 1.0 / math.sqrt(HEAD_DIM)

    def per_tile(tile_index):
        first_row = tile_index * tile_rows
        query_tile = lax.dynamic_slice_in_dim(query_view, first_row, tile_rows, 0)
        query_pos = first_row + jnp.arange(tile_rows, dtype=jnp.int32)
        query_doc = lax.dynamic_slice_in_dim(token_doc, first_row, tile_rows, 0)
        scores = jnp.einsum('qcgd,kcd->cgqk', query_tile, key_view) * score_scale
        allowed = (query_doc[:, None] == token_doc[None, :]) & (key_pos[None, :] <= query_pos[:, None])
        scores = jnp.where(allowed, scores, neg_fill)
        row_max = scores.max(-1, keepdims=True)
        weights = jnp.where(allowed, jnp.exp(scores - row_max), 0.0)
        totals = weights.sum(-1)
        rounded = lax.optimization_barrier(weights.astype(jnp.bfloat16))
        mixed = jnp.einsum('cgqk,kcd->qcgd', rounded.astype(jnp.float32), value_view)
        attended = mixed / jnp.transpose(totals, (2, 0, 1))[..., None]
        return attended.astype(jnp.bfloat16).reshape(tile_rows, HEADS * HEAD_DIM)
    tile_out = lax.map(per_tile, jnp.arange(seq_rows // tile_rows, dtype=jnp.int32))
    return tile_out.reshape(seq_rows, HEADS * HEAD_DIM)

def reference(queries, keys_values, doc_blocks, route_plan, out_weight):
    flat_marks = route_plan.reshape(NB).astype(jnp.int32)
    groups = jnp.arange(N_DP, dtype=jnp.int32)[:, None]
    source = jnp.bitwise_xor(groups, flat_marks[None, :])
    places = jnp.broadcast_to(jnp.arange(NB, dtype=jnp.int32)[None, :], (N_DP, NB))
    moved_query = queries.reshape(N_DP, NB, BLOCK, HEADS * HEAD_DIM)[source, places]
    moved_query = moved_query.reshape(N_DP, SEQ_LEN, HEADS * HEAD_DIM)
    moved_pairs = keys_values.reshape(N_DP, NB, BLOCK, KV_HEADS * 2 * HEAD_DIM)[source, places]
    moved_pairs = moved_pairs.reshape(N_DP, SEQ_LEN, KV_HEADS * 2 * HEAD_DIM)

    def one_group(inputs):
        query_rows, pair_rows, doc_ids = inputs
        attended = attend_group(query_rows, pair_rows, doc_ids)
        return jnp.dot(attended, out_weight, preferred_element_type=jnp.float32).astype(jnp.bfloat16)
    return lax.map(one_group, (moved_query, moved_pairs, doc_blocks))
```

```python
import functools
import math

import jax
import jax.numpy as jnp
from jax import lax
from jax.experimental import pallas as pl
from jax.experimental.pallas import tpu as pltpu
from jax.sharding import PartitionSpec as P

HEAD_DIM = 128
BLOCK = 128
GROUPS = 4
GQ = 512
GK = 256
GW = GQ + GK
TILE = 4
PAD = TILE - 1
NB = 32
NEG = -1e30

PAIRS = ((1, 4), (3, 4), (2, 4), (1, 3), (1, 7), (3, 5))


def plan_kernel(marks_ref, plan_ref):
    marks = [marks_ref[0, j] for j in range(4)]
    codes = [m >> 1 for m in marks]

    def cost(a, b):
        lo = jnp.minimum(codes[a], codes[b])
        hi = jnp.maximum(codes[a], codes[b])
        which = jnp.int32(0)
        for n, (u, v) in enumerate(PAIRS):
            which = jnp.where((lo == u) & (hi == v), n + 1, which)
        price = jnp.where(hi == 0, 0, jnp.where((which > 0) | (lo == 0), 1, 2))
        first = jnp.where(which > 0, which, jnp.where(hi > 0, len(PAIRS) + hi, 0))
        second = jnp.where(which > 0, 0, lo)
        swap = codes[a] > codes[b]
        return price, first, second, jnp.where(swap, b, a), jnp.where(swap, a, b)

    best = None
    for (a, b), (c, d) in (((0, 1), (2, 3)), ((0, 2), (1, 3)), ((0, 3), (1, 2))):
        one, two = cost(a, b), cost(c, d)
        total = one[0] + two[0]
        row = [total, one[3], one[4], two[3], two[4], one[1], one[2], two[1], two[2]]
        if best is None:
            best = row
        else:
            better = total < best[0]
            best = [jnp.where(better, n, o) for n, o in zip(row, best)]
    for n in range(8):
        plan_ref[0, n] = best[n + 1]
    for n in range(4):
        slot = best[n + 1]
        bit = jnp.int32(0)
        for j in range(4):
            bit = jnp.where(slot == j, marks[j] & 1, bit)
        plan_ref[0, 8 + n] = bit
    for n in range(12, 16):
        plan_ref[0, n] = jnp.int32(0)


def make_plan(route_plan):
    return pl.pallas_call(
        plan_kernel,
        out_shape=jax.ShapeDtypeStruct((1, 16), jnp.int32),
        in_specs=[pl.BlockSpec(memory_space=pltpu.SMEM)],
        out_specs=pl.BlockSpec(memory_space=pltpu.SMEM),
        name="plan",
    )(route_plan)


def prep_kernel(plan_ref, q_ref, qs_ref, k_ref, ks_ref, *out_refs):
    for n, out in enumerate(out_refs):
        rows = pl.ds(pl.multiple_of(plan_ref[0, n] * BLOCK, BLOCK), BLOCK)

        @pl.when(plan_ref[0, 8 + n] == 0)
        def _():
            out[0, :, :GQ] = q_ref[rows, :]
            out[0, :, GQ:] = k_ref[rows, :]

        @pl.when(plan_ref[0, 8 + n] != 0)
        def _():
            out[0, :, :GQ] = qs_ref[rows, :]
            out[0, :, GQ:] = ks_ref[rows, :]


def prep(plan, q, qs, kv, kvs):
    rows = q.shape[0]
    q_spec = pl.BlockSpec((rows, GQ), lambda c, p: (0, c))
    k_spec = pl.BlockSpec((rows, GK), lambda c, p: (0, c))
    o_spec = pl.BlockSpec((1, BLOCK, GW), lambda c, p: (c, 0, 0))
    return pl.pallas_call(
        prep_kernel,
        out_shape=[jax.ShapeDtypeStruct((GROUPS, BLOCK, GW), q.dtype)] * 4,
        grid_spec=pltpu.PrefetchScalarGridSpec(
            num_scalar_prefetch=1,
            grid=(GROUPS,),
            in_specs=[q_spec, q_spec, k_spec, k_spec],
            out_specs=[o_spec] * 4,
        ),
        name="prep",
    )(plan, q, qs, kv, kvs)


def flip(value):
    return [(i, i ^ value) for i in range(16)]


def send(block, code):
    return lax.ppermute(block, "dp", flip(code << 1))


def first_branches():
    yield lambda a, b: (a, b)
    for u, v in PAIRS:
        yield lambda a, b, u=u, v=v: (send(a, u), send(b, v))
    for v in range(1, 8):
        yield lambda a, b, v=v: (a, send(b, v))


def second_branches():
    yield lambda a: a
    for u in range(1, 8):
        yield lambda a, u=u: send(a, u)


def z_shift(x, k):
    moves = [(s, (((s // 2) + k) % 4) * 2 + s % 2) for s in range(8)]
    return lax.ppermute(x, "seq", moves)


def attend_kernel(where_ref, plans_ref, docs_ref, *refs):
    own = refs[0:8]
    other = refs[8:10]
    outs = refs[10:14]
    q_all, k_all, vt_all = refs[14:]
    z, h = where_ref[0], where_ref[1]

    k_all[pl.ds(0, PAD * BLOCK), :] = jnp.zeros((PAD * BLOCK, HEAD_DIM), k_all.dtype)
    vt_all[pl.ds(0, PAD)] = jnp.zeros((PAD, HEAD_DIM, BLOCK), vt_all.dtype)

    def put_kv(place, kv):
        k_all[pl.ds(pl.multiple_of((place + PAD) * BLOCK, BLOCK), BLOCK), :] = kv[:, :HEAD_DIM]
        vt_all[place + PAD] = kv[:, HEAD_DIM:].T

    for t in range(2):
        for k in range(4):
            zs = (z + 4 - k) % 4
            for i in range(2):
                slot = plans_ref[zs * 2 + h, 2 * t + i]
                piece = own[t * 4 + k]
                q = piece[i, :, :GQ]
                for g in range(4):
                    q_all[zs * 4 + slot, g * BLOCK : (g + 1) * BLOCK, :] = q[
                        :, g * HEAD_DIM : (g + 1) * HEAD_DIM
                    ]
                put_kv((zs * 2 + h) * 4 + slot, piece[i, :, GQ:])
                slot = plans_ref[zs * 2 + 1 - h, 2 * t + i]
                put_kv((zs * 2 + 1 - h) * 4 + slot, other[t][k, i])

    factor = math.log2(math.e) / math.sqrt(HEAD_DIM)
    keys = TILE * BLOCK
    lanes = 4 * BLOCK
    key_row = lax.broadcasted_iota(jnp.int32, (keys, lanes), 0)
    query_row = lax.broadcasted_iota(jnp.int32, (keys, lanes), 1) % BLOCK
    causal = key_row - PAD * BLOCK <= query_row

    for k in range(4):
        zd = (z + k) % 4

        def per_block(j, _, k=k, zd=zd):
            place = (zd * 2 + h) * 4 + j
            doc = docs_ref[0, place]
            start = lax.fori_loop(
                0, NB, lambda n, c: c + jnp.where(docs_ref[0, n] < doc, 1, 0), jnp.int32(0)
            )
            q = q_all[zd * 4 + j]

            def tile(n, state, first):
                top, total, acc = state
                base = place - n * TILE
                kt = k_all[pl.ds(pl.multiple_of(base * BLOCK, BLOCK), keys), :]
                s = lax.dot_general(
                    kt, q, (((1,), (1,)), ((), ())), preferred_element_type=jnp.float32
                )
                ok = key_row >= (start + PAD - base) * BLOCK
                if first:
                    ok = ok & causal
                s = jnp.where(ok, s, NEG)
                peak = jnp.max(s, axis=0, keepdims=True)
                if not first:
                    peak = jnp.maximum(peak, top)
                w = jnp.exp2((s - peak) * factor)
                w_sum = jnp.sum(w, axis=0, keepdims=True)
                vt = jnp.concatenate([vt_all[base + u] for u in range(TILE)], axis=1)
                mixed = jnp.dot(vt, w.astype(jnp.bfloat16), preferred_element_type=jnp.float32)
                if first:
                    return peak, w_sum, mixed
                keep = jnp.exp2((top - peak) * factor)
                return peak, total * keep + w_sum, acc * keep + mixed

            state = tile(0, (None, None, None), True)
            count = (place - start) // TILE + 1
            top, total, acc = lax.fori_loop(
                1, count, lambda n, state: tile(n, state, False), state
            )
            done = acc / total
            rows = pl.ds(pl.multiple_of(j * BLOCK, BLOCK), BLOCK)
            for g in range(4):
                outs[k][rows, g * HEAD_DIM : (g + 1) * HEAD_DIM] = done[
                    :, g * BLOCK : (g + 1) * BLOCK
                ].T.astype(jnp.bfloat16)
            return 0

        lax.fori_loop(0, 4, per_block, 0)


def attend(where, plans, docs, own, other):
    vmem = pl.BlockSpec(memory_space=pltpu.VMEM)
    smem = pl.BlockSpec(memory_space=pltpu.SMEM)
    return pl.pallas_call(
        attend_kernel,
        out_shape=[jax.ShapeDtypeStruct((4 * BLOCK, GQ), jnp.bfloat16)] * 4,
        in_specs=[smem] * 3 + [vmem] * 10,
        out_specs=[vmem] * 4,
        scratch_shapes=[
            pltpu.VMEM((16, 4 * BLOCK, HEAD_DIM), jnp.bfloat16),
            pltpu.VMEM(((NB + PAD) * BLOCK, HEAD_DIM), jnp.bfloat16),
            pltpu.VMEM((NB + PAD, HEAD_DIM, BLOCK), jnp.bfloat16),
        ],
        name="attend",
    )(where, plans, docs, *own, *other)


def body(queries, keys_values, doc_blocks, route_plan, out_weight):
    seq = lax.axis_index("seq")
    z, h = seq // 2, seq % 2
    q, kv = queries[0], keys_values[0]
    qs = lax.ppermute(q, "dp", flip(1))
    kvs = lax.ppermute(kv, "dp", flip(1))
    plan = make_plan(route_plan)
    plans = lax.all_gather(plan, "seq", axis=0, tiled=True)
    blocks = prep(plan, q, qs, kv, kvs)

    own, other = [], []
    for t in range(2):
        a, b = blocks[2 * t], blocks[2 * t + 1]
        a, b = lax.switch(plan[0, 4 + 2 * t], list(first_branches()), a, b)
        a = lax.switch(plan[0, 5 + 2 * t], list(second_branches()), a)
        pieces = []
        for k in range(4):
            c = (z + k) % 4
            piece = jnp.stack([lax.dynamic_index_in_dim(x, c, 0, keepdims=False) for x in (a, b)])
            pieces.append(piece if k == 0 else z_shift(piece, k))
        own += pieces
        mine = jnp.stack([piece[:, :, GQ:] for piece in pieces])
        other.append(lax.ppermute(mine, "seq", [(s, s ^ 1) for s in range(8)]))

    where = jnp.stack([z, h]).astype(jnp.int32)
    outs = attend(where, plans, doc_blocks, own, other)
    parts = [outs[0]] + [z_shift(outs[k], k) for k in range(1, 4)]
    stacked = jnp.stack(parts)
    attended = jnp.concatenate(
        [lax.dynamic_index_in_dim(stacked, (z + 4 - c) % 4, 0, keepdims=False) for c in range(4)], axis=1
    )
    weight = lax.all_gather(out_weight, "dp", axis=0, tiled=True)
    out = jnp.dot(attended, weight, preferred_element_type=jnp.float32)
    return out.astype(jnp.bfloat16)[None]


def solution(mesh):
    in_specs = (
        P("dp", "seq", None),
        P("dp", "seq", None),
        P("dp", None),
        P("seq", None),
        P("dp", None),
    )
    out_specs = P("dp", "seq", None)
    return jax.shard_map(body, mesh=mesh, in_specs=in_specs, out_specs=out_specs, check_vma=False)
```

```python
import math

import jax
import jax.numpy as jnp
from jax import lax
from jax.experimental import pallas as pl
from jax.experimental.pallas import tpu as pltpu
from jax.sharding import PartitionSpec as P

HEAD_DIM = 128
BLOCK = 128
GROUPS = 4
GQ = 512
GK = 256
GW = GQ + GK
TILE = 4
PAD = TILE - 1
NB = 32
NEG = -1e30


def prep_kernel(z_ref, marks_ref, q_ref, qs_ref, k_ref, ks_ref, *out_refs):
    for j, out in enumerate(out_refs):
        rows = slice(j * BLOCK, (j + 1) * BLOCK)

        @pl.when(marks_ref[0, j] % 2 == 0)
        def _():
            out[0, :, :GQ] = q_ref[rows, :]
            out[0, :, GQ:] = k_ref[rows, :]

        @pl.when(marks_ref[0, j] % 2 != 0)
        def _():
            out[0, :, :GQ] = qs_ref[rows, :]
            out[0, :, GQ:] = ks_ref[rows, :]


def prep(z, marks, q, qs, kv, kvs):
    rows = q.shape[0]
    blocks = rows // BLOCK
    q_spec = pl.BlockSpec((rows, GQ), lambda k, z, m: (0, (z[0] + k) % GROUPS))
    k_spec = pl.BlockSpec((rows, GK), lambda k, z, m: (0, (z[0] + k) % GROUPS))
    o_spec = pl.BlockSpec((1, BLOCK, GW), lambda k, z, m: (k, 0, 0))
    return pl.pallas_call(
        prep_kernel,
        out_shape=[jax.ShapeDtypeStruct((GROUPS, BLOCK, GW), q.dtype)] * blocks,
        grid_spec=pltpu.PrefetchScalarGridSpec(
            num_scalar_prefetch=2,
            grid=(GROUPS,),
            in_specs=[q_spec, q_spec, k_spec, k_spec],
            out_specs=[o_spec] * blocks,
        ),
        name="prep",
    )(z, marks, q, qs, kv, kvs)


def flip(value):
    return [(i, i ^ value) for i in range(16)]


def moves():
    yield lambda x: x
    for code in range(1, 8):
        yield lambda x, code=code: lax.ppermute(x, "dp", flip(code << 1))


def z_shift(x, k):
    return lax.ppermute(x, "seq", [(s, (((s // 2) + k) % 4) * 2 + s % 2) for s in range(8)])


def attend_kernel(where_ref, docs_ref, *refs):
    own = [[refs[j]] + [refs[4 + 3 * j + k] for k in range(3)] for j in range(4)]
    other = refs[16:20]
    outs = refs[20:24]
    q_all, k_all, vt_all = refs[24:]
    z, h = where_ref[0], where_ref[1]

    k_all[pl.ds(0, PAD * BLOCK), :] = jnp.zeros((PAD * BLOCK, HEAD_DIM), k_all.dtype)
    vt_all[pl.ds(0, PAD)] = jnp.zeros((PAD, HEAD_DIM, BLOCK), vt_all.dtype)

    def put_kv(place, kv):
        k_all[pl.ds(pl.multiple_of((place + PAD) * BLOCK, BLOCK), BLOCK), :] = kv[:, :HEAD_DIM]
        vt_all[place + PAD] = kv[:, HEAD_DIM:].T

    for j in range(4):
        for k in range(4):
            zs = (z + 4 - k) % 4
            piece = own[j][k][0] if k == 0 else own[j][k][...]
            for g in range(4):
                q_all[zs * 4 + j, g * BLOCK : (g + 1) * BLOCK, :] = piece[
                    :, g * HEAD_DIM : (g + 1) * HEAD_DIM
                ]
            put_kv((zs * 2 + h) * 4 + j, piece[:, GQ:])
            put_kv((zs * 2 + 1 - h) * 4 + j, other[j][k])

    factor = math.log2(math.e) / math.sqrt(HEAD_DIM)
    keys = TILE * BLOCK
    lanes = 2 * BLOCK
    key_row = lax.broadcasted_iota(jnp.int32, (BLOCK, lanes), 0)
    query_row = lax.broadcasted_iota(jnp.int32, (BLOCK, lanes), 1) % BLOCK
    causal = key_row <= query_row

    for k in range(4):
        zd = (z + k) % 4

        def per_block(j, _, k=k, zd=zd):
            place = (zd * 2 + h) * 4 + j
            doc = docs_ref[0, place]
            start = lax.fori_loop(
                0, NB, lambda n, c: c + jnp.where(docs_ref[0, n] < doc, 1, 0), jnp.int32(0)
            )
            qs = [q_all[zd * 4 + j, i * lanes : (i + 1) * lanes, :] for i in range(2)]

            def tile(n, states, first):
                base = place - n * TILE
                kt = k_all[pl.ds(pl.multiple_of(base * BLOCK, BLOCK), keys), :]
                vt = jnp.concatenate([vt_all[base + u] for u in range(TILE)], axis=1)
                new = []
                for q, state in zip(qs, states):
                    s = lax.dot_general(
                        kt, q, (((1,), (1,)), ((), ())), preferred_element_type=jnp.float32
                    )
                    parts = []
                    for u in range(TILE):
                        part = s[u * BLOCK : (u + 1) * BLOCK]
                        if first and u == TILE - 1:
                            part = jnp.where(causal, part, NEG)
                        else:
                            part = jnp.where(base + u >= start + PAD, part, NEG)
                        parts.append(part)
                    s = jnp.concatenate(parts, axis=0)
                    peak = jnp.max(s, axis=0, keepdims=True)
                    if not first:
                        peak = jnp.maximum(peak, state[0])
                    w = jnp.exp2((s - peak) * factor)
                    w_sum = jnp.sum(w, axis=0, keepdims=True)
                    mixed = jnp.dot(vt, w.astype(jnp.bfloat16), preferred_element_type=jnp.float32)
                    if first:
                        new.append((peak, w_sum, mixed))
                    else:
                        keep = jnp.exp2((state[0] - peak) * factor)
                        new.append((peak, state[1] * keep + w_sum, state[2] * keep + mixed))
                return tuple(new)

            states = tile(0, (None, None), True)
            count = (place - start) // TILE + 1
            states = lax.fori_loop(1, count, lambda n, st: tile(n, st, False), states)
            rows = pl.ds(pl.multiple_of(j * BLOCK, BLOCK), BLOCK)
            for i, (_, total, acc) in enumerate(states):
                done = acc / total
                for g in range(2):
                    cols = (2 * i + g) * HEAD_DIM
                    outs[k][rows, cols : cols + HEAD_DIM] = done[
                        :, g * BLOCK : (g + 1) * BLOCK
                    ].T.astype(jnp.bfloat16)
            return 0

        lax.fori_loop(0, 4, per_block, 0)


def attend(where, docs, blocks, pieces, other):
    vmem = pl.BlockSpec(memory_space=pltpu.VMEM)
    smem = pl.BlockSpec(memory_space=pltpu.SMEM)
    first = pl.BlockSpec((1, BLOCK, GW), lambda i: (0, 0, 0))
    return pl.pallas_call(
        attend_kernel,
        grid=(1,),
        out_shape=[jax.ShapeDtypeStruct((4 * BLOCK, GQ), jnp.bfloat16)] * 4,
        in_specs=[smem] * 2 + [first] * 4 + [vmem] * 16,
        out_specs=[vmem] * 4,
        scratch_shapes=[
            pltpu.VMEM((16, 4 * BLOCK, HEAD_DIM), jnp.bfloat16),
            pltpu.VMEM(((NB + PAD) * BLOCK, HEAD_DIM), jnp.bfloat16),
            pltpu.VMEM((NB + PAD, HEAD_DIM, BLOCK), jnp.bfloat16),
        ],
        name="attend",
    )(where, docs, *blocks, *pieces, *other)


def tie_kernel(w_ref, token_ref, out_ref, sem):
    copy = pltpu.make_async_copy(w_ref, out_ref, sem)
    copy.start()
    copy.wait()


def tie(weight, token):
    any_spec = pl.BlockSpec(memory_space=pl.ANY)
    return pl.pallas_call(
        tie_kernel,
        out_shape=jax.ShapeDtypeStruct(weight.shape, weight.dtype),
        in_specs=[any_spec] * 2,
        out_specs=any_spec,
        scratch_shapes=[pltpu.SemaphoreType.DMA],
        name="tie",
    )(weight, token)


def body(queries, keys_values, doc_blocks, route_plan, out_weight):
    seq = lax.axis_index("seq")
    z, h = seq >> 1, seq & 1
    q, kv = queries[0], keys_values[0]
    qs = lax.ppermute(q, "dp", flip(1))
    kvs = lax.ppermute(kv, "dp", flip(1))
    where = jnp.stack([z, h]).astype(jnp.int32)
    blocks = list(prep(where, route_plan, q, qs, kv, kvs))

    pieces, other = [], []
    for j in range(4):
        block = lax.switch(route_plan[0, j] >> 1, list(moves()), blocks[j])
        blocks[j] = block
        came = []
        for k in range(1, 4):
            came.append(z_shift(block[k], k))
        pieces += came
        mine = jnp.stack([block[0, :, GQ:]] + [piece[:, GQ:] for piece in came])
        other.append(lax.ppermute(mine, "seq", [(s, s ^ 1) for s in range(8)]))
    weight = lax.all_gather(tie(out_weight, blocks[3]), "dp", axis=0, tiled=True)

    outs = attend(where, doc_blocks, blocks, pieces, other)
    parts = [outs[0]] + [z_shift(outs[k], k) for k in range(1, 4)]
    stacked = jnp.stack(parts)
    attended = jnp.concatenate(
        [lax.dynamic_index_in_dim(stacked, (z + 4 - c) & 3, 0, keepdims=False) for c in range(4)],
        axis=1,
    )
    out = jnp.dot(attended, weight, preferred_element_type=jnp.float32)
    return out.astype(jnp.bfloat16)[None]


def solution(mesh):
    in_specs = (
        P("dp", "seq", None),
        P("dp", "seq", None),
        P("dp", None),
        P("seq", None),
        P("dp", None),
    )
    out_specs = P("dp", "seq", None)

    return jax.shard_map(body, mesh=mesh, in_specs=in_specs, out_specs=out_specs, check_vma=False)
```

```python
import math

import jax
import jax.numpy as jnp
from jax import lax
from jax.experimental import pallas as pl
from jax.experimental.pallas import tpu as pltpu
from jax.sharding import PartitionSpec as P

HEAD_DIM = 128
BLOCK = 128
GROUPS = 4
GQ = 512
GK = 256
GW = GQ + GK
TILE = 2
PAD = TILE - 1
CHAINS = 1
NB = 32
NEG = -1e30


def prep_kernel(z_ref, marks_ref, q_ref, qs_ref, k_ref, ks_ref, *out_refs):
    for j, out in enumerate(out_refs):
        rows = slice(j * BLOCK, (j + 1) * BLOCK)

        @pl.when(marks_ref[0, j] % 2 == 0)
        def _():
            out[0, :, :GQ] = q_ref[rows, :]
            out[0, :, GQ:] = k_ref[rows, :]

        @pl.when(marks_ref[0, j] % 2 != 0)
        def _():
            out[0, :, :GQ] = qs_ref[rows, :]
            out[0, :, GQ:] = ks_ref[rows, :]


def prep(z, marks, q, qs, kv, kvs):
    rows = q.shape[0]
    blocks = rows // BLOCK
    q_spec = pl.BlockSpec((rows, GQ), lambda k, z, m: (0, (z[0] + k) % GROUPS))
    k_spec = pl.BlockSpec((rows, GK), lambda k, z, m: (0, (z[0] + k) % GROUPS))
    o_spec = pl.BlockSpec((1, BLOCK, GW), lambda k, z, m: (k, 0, 0))
    return pl.pallas_call(
        prep_kernel,
        out_shape=[jax.ShapeDtypeStruct((GROUPS, BLOCK, GW), q.dtype)] * blocks,
        grid_spec=pltpu.PrefetchScalarGridSpec(
            num_scalar_prefetch=2,
            grid=(GROUPS,),
            in_specs=[q_spec, q_spec, k_spec, k_spec],
            out_specs=[o_spec] * blocks,
        ),
        name="prep",
    )(z, marks, q, qs, kv, kvs)


def flip(value):
    return [(i, i ^ value) for i in range(16)]


def moves():
    yield lambda x: x
    for code in range(1, 8):
        yield lambda x, code=code: lax.ppermute(x, "dp", flip(code << 1))


def z_shift(x, k):
    return lax.ppermute(x, "seq", [(s, (((s // 2) + k) % 4) * 2 + s % 2) for s in range(8)])


def attend_kernel(where_ref, starts_ref, *refs):
    own = [[refs[j]] + [refs[4 + 3 * j + k] for k in range(3)] for j in range(4)]
    other = refs[16:20]
    outs = refs[20:24]
    q_all, k_all, vt_all = refs[24:]
    z, h = where_ref[0], where_ref[1]

    k_all[pl.ds(0, PAD * BLOCK), :] = jnp.zeros((PAD * BLOCK, HEAD_DIM), k_all.dtype)
    vt_all[pl.ds(0, PAD)] = jnp.zeros((PAD, HEAD_DIM, BLOCK), vt_all.dtype)

    def put_kv(place, kv):
        k_all[pl.ds(pl.multiple_of((place + PAD) * BLOCK, BLOCK), BLOCK), :] = kv[:, :HEAD_DIM]
        vt_all[place + PAD] = kv[:, HEAD_DIM:].T

    for j in range(4):
        for k in range(4):
            zs = (z + 4 - k) % 4
            piece = own[j][k][0] if k == 0 else own[j][k][...]
            for g in range(4):
                q_all[zs * 4 + j, g * BLOCK : (g + 1) * BLOCK, :] = piece[
                    :, g * HEAD_DIM : (g + 1) * HEAD_DIM
                ]
            put_kv((zs * 2 + h) * 4 + j, piece[:, GQ:])
            put_kv((zs * 2 + 1 - h) * 4 + j, other[j][k])

    factor = math.log2(math.e) / math.sqrt(HEAD_DIM)
    keys = TILE * BLOCK
    lanes = 4 // CHAINS * BLOCK
    key_row = lax.broadcasted_iota(jnp.int32, (BLOCK, lanes), 0)
    query_row = lax.broadcasted_iota(jnp.int32, (BLOCK, lanes), 1) % BLOCK
    causal = key_row <= query_row

    for k in range(4):
        zd = (z + k) % 4

        def per_block(j, _, k=k, zd=zd):
            place = (zd * 2 + h) * 4 + j
            start = starts_ref[0, place]
            qs = [q_all[zd * 4 + j, i * lanes : (i + 1) * lanes, :] for i in range(CHAINS)]

            def tile(n, states, first):
                base = place - n * TILE
                kt = k_all[pl.ds(pl.multiple_of(base * BLOCK, BLOCK), keys), :]
                vt = jnp.concatenate([vt_all[base + u] for u in range(TILE)], axis=1)
                new = []
                for q, state in zip(qs, states):
                    s = lax.dot_general(
                        kt, q, (((1,), (1,)), ((), ())), preferred_element_type=jnp.float32
                    )
                    parts = []
                    for u in range(TILE):
                        part = s[u * BLOCK : (u + 1) * BLOCK]
                        if first and u == TILE - 1:
                            part = jnp.where(causal, part, NEG)
                        else:
                            part = jnp.where(base + u >= start + PAD, part, NEG)
                        parts.append(part)
                    s = jnp.concatenate(parts, axis=0)
                    peak = jnp.max(s, axis=0, keepdims=True)
                    if not first:
                        peak = jnp.maximum(peak, state[0])
                    w = jnp.exp2((s - peak) * factor)
                    w_sum = jnp.sum(w, axis=0, keepdims=True)
                    mixed = jnp.dot(vt, w.astype(jnp.bfloat16), preferred_element_type=jnp.float32)
                    if first:
                        new.append((peak, w_sum, mixed))
                    else:
                        keep = jnp.exp2((state[0] - peak) * factor)
                        new.append((peak, state[1] * keep + w_sum, state[2] * keep + mixed))
                return tuple(new)

            states = tile(0, (None,) * CHAINS, True)
            count = (place - start) // TILE + 1
            states = lax.fori_loop(1, count, lambda n, st: tile(n, st, False), states)
            rows = pl.ds(pl.multiple_of(j * BLOCK, BLOCK), BLOCK)
            for i, (_, total, acc) in enumerate(states):
                done = acc / total
                for g in range(4 // CHAINS):
                    cols = (4 // CHAINS * i + g) * HEAD_DIM
                    outs[k][rows, cols : cols + HEAD_DIM] = done[
                        :, g * BLOCK : (g + 1) * BLOCK
                    ].T.astype(jnp.bfloat16)
            return 0

        lax.fori_loop(0, 4, per_block, 0)


def attend(where, starts, blocks, pieces, other):
    vmem = pl.BlockSpec(memory_space=pltpu.VMEM)
    smem = pl.BlockSpec(memory_space=pltpu.SMEM)
    first = pl.BlockSpec((1, BLOCK, GW), lambda i: (0, 0, 0))
    return pl.pallas_call(
        attend_kernel,
        grid=(1,),
        out_shape=[jax.ShapeDtypeStruct((4 * BLOCK, GQ), jnp.bfloat16)] * 4,
        in_specs=[smem] * 2 + [first] * 4 + [vmem] * 16,
        out_specs=[vmem] * 4,
        scratch_shapes=[
            pltpu.VMEM((16, 4 * BLOCK, HEAD_DIM), jnp.bfloat16),
            pltpu.VMEM(((NB + PAD) * BLOCK, HEAD_DIM), jnp.bfloat16),
            pltpu.VMEM((NB + PAD, HEAD_DIM, BLOCK), jnp.bfloat16),
        ],
        name="attend",
    )(where, starts, *blocks, *pieces, *other)


def collect_kernel(*refs):
    out = refs[-1]
    out[0] = refs[0][0]
    for k in range(1, GROUPS):
        out[k] = refs[k][...]


def collect(block, came):
    first = pl.BlockSpec((1, BLOCK, GK), lambda i: (0, 0, GQ // GK))
    rest = pl.BlockSpec((BLOCK, GK), lambda i: (0, GQ // GK))
    return pl.pallas_call(
        collect_kernel,
        grid=(1,),
        out_shape=jax.ShapeDtypeStruct((GROUPS, BLOCK, GK), block.dtype),
        in_specs=[first] + [rest] * 3,
        out_specs=pl.BlockSpec((GROUPS, BLOCK, GK), lambda i: (0, 0, 0)),
        name="collect",
    )(block, *came)


def tie_kernel(w_ref, token_ref, out_ref):
    out_ref[...] = w_ref[...]


def tie(weight, token):
    rows, cols = weight.shape
    spec = pl.BlockSpec((rows, cols // 2), lambda i: (0, i))
    return pl.pallas_call(
        tie_kernel,
        grid=(2,),
        out_shape=jax.ShapeDtypeStruct(weight.shape, weight.dtype),
        in_specs=[spec, pl.BlockSpec(memory_space=pl.ANY)],
        out_specs=spec,
        name="tie",
    )(weight, token)


def body(queries, keys_values, doc_blocks, route_plan, out_weight):
    seq = lax.axis_index("seq")
    z, h = seq >> 1, seq & 1
    q, kv = queries[0], keys_values[0]
    qs = lax.ppermute(q, "dp", flip(1))
    kvs = lax.ppermute(kv, "dp", flip(1))
    where = jnp.stack([z, h]).astype(jnp.int32)
    docs = doc_blocks[0]
    starts = jnp.sum((docs[None, :] < docs[:, None]).astype(jnp.int32), axis=1)[None]
    blocks = list(prep(where, route_plan, q, qs, kv, kvs))

    pieces, other = [], []
    for j in range(4):
        block = lax.switch(route_plan[0, j] >> 1, list(moves()), blocks[j])
        blocks[j] = block
        came = []
        for k in range(1, 4):
            came.append(z_shift(block[k], k))
        pieces += came
        mine = collect(block, came)
        other.append(lax.ppermute(mine, "seq", [(s, s ^ 1) for s in range(8)]))
    weight = lax.all_gather(tie(out_weight, blocks[2]), "dp", axis=0, tiled=True)

    outs = attend(where, starts, blocks, pieces, other)
    parts = [outs[0]] + [z_shift(outs[k], k) for k in range(1, 4)]
    stacked = jnp.stack(parts)
    attended = jnp.concatenate(
        [lax.dynamic_index_in_dim(stacked, (z + 4 - c) & 3, 0, keepdims=False) for c in range(4)],
        axis=1,
    )
    out = jnp.dot(attended, weight, preferred_element_type=jnp.float32)
    return out.astype(jnp.bfloat16)[None]


def solution(mesh):
    in_specs = (
        P("dp", "seq", None),
        P("dp", "seq", None),
        P("dp", None),
        P("seq", None),
        P("dp", None),
    )
    out_specs = P("dp", "seq", None)

    return jax.shard_map(body, mesh=mesh, in_specs=in_specs, out_specs=out_specs, check_vma=False)
```

```python
import math

import jax
import jax.numpy as jnp
from jax import lax
from jax.experimental import pallas as pl
from jax.experimental.pallas import tpu as pltpu
from jax.sharding import PartitionSpec as P

HEAD_DIM = 128
BLOCK = 128
GROUPS = 4
GQ = 512
GK = 256
GW = GQ + GK
TILE = 2
PAD = TILE - 1
CHAINS = 1
NB = 32
NEG = -1e30


def prep_kernel(z_ref, marks_ref, q_ref, qs_ref, k_ref, ks_ref, *out_refs):
    for j, out in enumerate(out_refs):
        rows = slice(j * BLOCK, (j + 1) * BLOCK)

        @pl.when(marks_ref[0, j] % 2 == 0)
        def _():
            out[0, :, :GQ] = q_ref[rows, :]
            out[0, :, GQ:] = k_ref[rows, :]

        @pl.when(marks_ref[0, j] % 2 != 0)
        def _():
            out[0, :, :GQ] = qs_ref[rows, :]
            out[0, :, GQ:] = ks_ref[rows, :]


def prep(z, marks, q, qs, kv, kvs):
    rows = q.shape[0]
    blocks = rows // BLOCK
    q_spec = pl.BlockSpec((rows, GQ), lambda k, z, m: (0, (z[0] + k) % GROUPS))
    k_spec = pl.BlockSpec((rows, GK), lambda k, z, m: (0, (z[0] + k) % GROUPS))
    o_spec = pl.BlockSpec((1, BLOCK, GW), lambda k, z, m: (k, 0, 0))
    return pl.pallas_call(
        prep_kernel,
        out_shape=[jax.ShapeDtypeStruct((GROUPS, BLOCK, GW), q.dtype)] * blocks,
        grid_spec=pltpu.PrefetchScalarGridSpec(
            num_scalar_prefetch=2,
            grid=(GROUPS,),
            in_specs=[q_spec, q_spec, k_spec, k_spec],
            out_specs=[o_spec] * blocks,
        ),
        name="prep",
    )(z, marks, q, qs, kv, kvs)


def flip(value):
    return [(i, i ^ value) for i in range(16)]


def moves():
    yield lambda x: x
    for code in range(1, 8):
        yield lambda x, code=code: lax.ppermute(x, "dp", flip(code << 1))


def z_shift(x, k):
    return lax.ppermute(x, "seq", [(s, (((s // 2) + k) % 4) * 2 + s % 2) for s in range(8)])


def attend_kernel(where_ref, starts_ref, *refs):
    own = [[refs[j]] + [refs[4 + 3 * j + k] for k in range(3)] for j in range(4)]
    other = refs[16:20]
    outs = refs[20:24]
    q_all, k_all, vt_all = refs[24:]
    z, h = where_ref[0], where_ref[1]

    k_all[pl.ds(0, PAD * BLOCK), :] = jnp.zeros((PAD * BLOCK, HEAD_DIM), k_all.dtype)
    vt_all[pl.ds(0, PAD)] = jnp.zeros((PAD, HEAD_DIM, BLOCK), vt_all.dtype)

    def put_kv(place, kv):
        k_all[pl.ds(pl.multiple_of((place + PAD) * BLOCK, BLOCK), BLOCK), :] = kv[:, :HEAD_DIM]
        vt_all[place + PAD] = kv[:, HEAD_DIM:].T

    for j in range(4):
        for k in range(4):
            zs = (z + 4 - k) % 4
            piece = own[j][k][0] if k == 0 else own[j][k][...]
            for g in range(4):
                q_all[zs * 4 + j, g * BLOCK : (g + 1) * BLOCK, :] = piece[
                    :, g * HEAD_DIM : (g + 1) * HEAD_DIM
                ]
            put_kv((zs * 2 + h) * 4 + j, piece[:, GQ:])
            put_kv((zs * 2 + 1 - h) * 4 + j, other[j][k])

    factor = math.log2(math.e) / math.sqrt(HEAD_DIM)
    keys = TILE * BLOCK
    lanes = 4 // CHAINS * BLOCK
    key_row = lax.broadcasted_iota(jnp.int32, (BLOCK, lanes), 0)
    query_row = lax.broadcasted_iota(jnp.int32, (BLOCK, lanes), 1) % BLOCK
    causal = key_row <= query_row

    for k in range(4):
        zd = (z + k) % 4

        def per_block(j, _, k=k, zd=zd):
            place = (zd * 2 + h) * 4 + j
            start = starts_ref[0, place]
            qs = [q_all[zd * 4 + j, i * lanes : (i + 1) * lanes, :] for i in range(CHAINS)]

            def tile(n, states, first):
                base = place - n * TILE
                kt = k_all[pl.ds(pl.multiple_of(base * BLOCK, BLOCK), keys), :]
                vt = jnp.concatenate([vt_all[base + u] for u in range(TILE)], axis=1)
                new = []
                for q, state in zip(qs, states):
                    s = lax.dot_general(
                        kt, q, (((1,), (1,)), ((), ())), preferred_element_type=jnp.float32
                    )
                    parts = []
                    for u in range(TILE):
                        part = s[u * BLOCK : (u + 1) * BLOCK]
                        if first and u == TILE - 1:
                            part = jnp.where(causal, part, NEG)
                        else:
                            part = jnp.where(base + u >= start + PAD, part, NEG)
                        parts.append(part)
                    s = jnp.concatenate(parts, axis=0)
                    peak = jnp.max(s, axis=0, keepdims=True)
                    if not first:
                        peak = jnp.maximum(peak, state[0])
                    w = jnp.exp2((s - peak) * factor)
                    w_sum = jnp.sum(w, axis=0, keepdims=True)
                    mixed = jnp.dot(vt, w.astype(jnp.bfloat16), preferred_element_type=jnp.float32)
                    if first:
                        new.append((peak, w_sum, mixed))
                    else:
                        keep = jnp.exp2((state[0] - peak) * factor)
                        new.append((peak, state[1] * keep + w_sum, state[2] * keep + mixed))
                return tuple(new)

            states = tile(0, (None,) * CHAINS, True)
            count = (place - start) // TILE + 1
            states = lax.fori_loop(1, count, lambda n, st: tile(n, st, False), states)
            rows = pl.ds(pl.multiple_of(j * BLOCK, BLOCK), BLOCK)
            for i, (_, total, acc) in enumerate(states):
                done = acc / total
                for g in range(4 // CHAINS):
                    cols = (4 // CHAINS * i + g) * HEAD_DIM
                    outs[k][rows, cols : cols + HEAD_DIM] = done[
                        :, g * BLOCK : (g + 1) * BLOCK
                    ].T.astype(jnp.bfloat16)
            return 0

        lax.fori_loop(0, 4, per_block, 0)


def attend(where, starts, blocks, pieces, other):
    vmem = pl.BlockSpec(memory_space=pltpu.VMEM)
    smem = pl.BlockSpec(memory_space=pltpu.SMEM)
    first = pl.BlockSpec((1, BLOCK, GW), lambda i: (0, 0, 0))
    return pl.pallas_call(
        attend_kernel,
        grid=(1,),
        out_shape=[jax.ShapeDtypeStruct((4 * BLOCK, GQ), jnp.bfloat16)] * 4,
        in_specs=[smem] * 2 + [first] * 4 + [vmem] * 16,
        out_specs=[vmem] * 4,
        scratch_shapes=[
            pltpu.VMEM((16, 4 * BLOCK, HEAD_DIM), jnp.bfloat16),
            pltpu.VMEM(((NB + PAD) * BLOCK, HEAD_DIM), jnp.bfloat16),
            pltpu.VMEM((NB + PAD, HEAD_DIM, BLOCK), jnp.bfloat16),
        ],
        name="attend",
    )(where, starts, *blocks, *pieces, *other)


def collect_kernel(*refs):
    out = refs[-1]
    out[0] = refs[0][0]
    for k in range(1, GROUPS):
        out[k] = refs[k][...]


def collect(block, came):
    first = pl.BlockSpec((1, BLOCK, GK), lambda i: (0, 0, GQ // GK))
    rest = pl.BlockSpec((BLOCK, GK), lambda i: (0, GQ // GK))
    return pl.pallas_call(
        collect_kernel,
        grid=(1,),
        out_shape=jax.ShapeDtypeStruct((GROUPS, BLOCK, GK), block.dtype),
        in_specs=[first] + [rest] * 3,
        out_specs=pl.BlockSpec((GROUPS, BLOCK, GK), lambda i: (0, 0, 0)),
        name="collect",
    )(block, *came)


def project_kernel(where_ref, *refs):
    parts, w_ref, out_ref, rows = refs[:4], refs[4], refs[5], refs[6]

    @pl.when(pl.program_id(0) == 0)
    def _():
        for k, part in enumerate(parts):
            group = (where_ref[0] + GROUPS - k) % GROUPS
            rows[:, pl.ds(pl.multiple_of(group * GQ, GQ), GQ)] = part[...]

    out_ref[...] = jnp.dot(rows[...], w_ref[...], preferred_element_type=jnp.float32).astype(
        out_ref.dtype
    )


def project(where, parts, weight):
    depth, cols = weight.shape
    count = parts[0].shape[0]
    wide = 512
    part = pl.BlockSpec((count, GQ), lambda i, w: (0, 0))
    return pl.pallas_call(
        project_kernel,
        out_shape=jax.ShapeDtypeStruct((count, cols), weight.dtype),
        grid_spec=pltpu.PrefetchScalarGridSpec(
            num_scalar_prefetch=1,
            grid=(cols // wide,),
            in_specs=[part] * 4 + [pl.BlockSpec((depth, wide), lambda i, w: (0, i))],
            out_specs=pl.BlockSpec((count, wide), lambda i, w: (0, i)),
            scratch_shapes=[pltpu.VMEM((count, depth), weight.dtype)],
        ),
        name="project",
    )(where, *parts, weight)


def tie_kernel(w_ref, token_ref, out_ref):
    out_ref[...] = w_ref[...]


def tie(weight, token):
    rows, cols = weight.shape
    spec = pl.BlockSpec((rows, cols // 2), lambda i: (0, i))
    return pl.pallas_call(
        tie_kernel,
        grid=(2,),
        out_shape=jax.ShapeDtypeStruct(weight.shape, weight.dtype),
        in_specs=[spec, pl.BlockSpec(memory_space=pl.ANY)],
        out_specs=spec,
        name="tie",
    )(weight, token)


def body(queries, keys_values, doc_blocks, route_plan, out_weight):
    seq = lax.axis_index("seq")
    z, h = seq >> 1, seq & 1
    q, kv = queries[0], keys_values[0]
    qs = lax.ppermute(q, "dp", flip(1))
    kvs = lax.ppermute(kv, "dp", flip(1))
    where = jnp.stack([z, h]).astype(jnp.int32)
    docs = doc_blocks[0]
    starts = jnp.sum((docs[None, :] < docs[:, None]).astype(jnp.int32), axis=1)[None]
    blocks = list(prep(where, route_plan, q, qs, kv, kvs))

    pieces, other = [], []
    for j in range(4):
        block = lax.switch(route_plan[0, j] >> 1, list(moves()), blocks[j])
        blocks[j] = block
        came = []
        for k in range(1, 4):
            came.append(z_shift(block[k], k))
        pieces += came
        mine = collect(block, came)
        other.append(lax.ppermute(mine, "seq", [(s, s ^ 1) for s in range(8)]))
    weight = lax.all_gather(tie(out_weight, blocks[2]), "dp", axis=0, tiled=True)

    outs = attend(where, starts, blocks, pieces, other)
    parts = [outs[0]] + [z_shift(outs[k], k) for k in range(1, 4)]
    return project(where, parts, weight)[None]


def solution(mesh):
    in_specs = (
        P("dp", "seq", None),
        P("dp", "seq", None),
        P("dp", None),
        P("seq", None),
        P("dp", None),
    )
    out_specs = P("dp", "seq", None)

    return jax.shard_map(body, mesh=mesh, in_specs=in_specs, out_specs=out_specs, check_vma=False)
```

```python
import math

import jax
import jax.numpy as jnp
from jax import lax
from jax.experimental import pallas as pl
from jax.experimental.pallas import tpu as pltpu
from jax.sharding import PartitionSpec as P

HEAD_DIM = 128
BLOCK = 128
GROUPS = 4
GQ = 512
GK = 256
GW = GQ + GK
TILE = 2
PAD = TILE - 1
CHAINS = 1
NB = 32
NEG = -1e30
COLS_A = 1536
WIDE = 512
XC = [list(range(8)), list(range(8, 16))]


def prep_kernel(z_ref, marks_ref, q_ref, qs_ref, k_ref, ks_ref, *out_refs):
    for j, out in enumerate(out_refs):
        rows = slice(j * BLOCK, (j + 1) * BLOCK)

        @pl.when(marks_ref[0, j] % 2 == 0)
        def _():
            out[0, :, :GQ] = q_ref[rows, :]
            out[0, :, GQ:] = k_ref[rows, :]

        @pl.when(marks_ref[0, j] % 2 != 0)
        def _():
            out[0, :, :GQ] = qs_ref[rows, :]
            out[0, :, GQ:] = ks_ref[rows, :]


def prep(z, marks, q, qs, kv, kvs):
    rows = q.shape[0]
    blocks = rows // BLOCK
    q_spec = pl.BlockSpec((rows, GQ), lambda k, z, m: (0, (z[0] + k) % GROUPS))
    k_spec = pl.BlockSpec((rows, GK), lambda k, z, m: (0, (z[0] + k) % GROUPS))
    o_spec = pl.BlockSpec((1, BLOCK, GW), lambda k, z, m: (k, 0, 0))
    return pl.pallas_call(
        prep_kernel,
        out_shape=[jax.ShapeDtypeStruct((GROUPS, BLOCK, GW), q.dtype)] * blocks,
        grid_spec=pltpu.PrefetchScalarGridSpec(
            num_scalar_prefetch=2,
            grid=(GROUPS,),
            in_specs=[q_spec, q_spec, k_spec, k_spec],
            out_specs=[o_spec] * blocks,
        ),
        name="prep",
    )(z, marks, q, qs, kv, kvs)


def flip(value):
    return [(i, i ^ value) for i in range(16)]


def moves():
    yield lambda x: x
    for code in range(1, 8):
        yield lambda x, code=code: lax.ppermute(x, "dp", flip(code << 1))


def z_shift(x, k):
    return lax.ppermute(x, "seq", [(s, (((s // 2) + k) % 4) * 2 + s % 2) for s in range(8)])


def attend_kernel(where_ref, starts_ref, *refs):
    own = [[refs[j]] + [refs[4 + 3 * j + k] for k in range(3)] for j in range(4)]
    other = refs[16:20]
    outs = refs[20:24]
    q_all, k_all, vt_all = refs[24:]
    z, h = where_ref[0], where_ref[1]

    k_all[pl.ds(0, PAD * BLOCK), :] = jnp.zeros((PAD * BLOCK, HEAD_DIM), k_all.dtype)
    vt_all[pl.ds(0, PAD)] = jnp.zeros((PAD, HEAD_DIM, BLOCK), vt_all.dtype)

    def put_kv(place, kv):
        k_all[pl.ds(pl.multiple_of((place + PAD) * BLOCK, BLOCK), BLOCK), :] = kv[:, :HEAD_DIM]
        vt_all[place + PAD] = kv[:, HEAD_DIM:].T

    for j in range(4):
        for k in range(4):
            zs = (z + 4 - k) % 4
            piece = own[j][k][0] if k == 0 else own[j][k][...]
            for g in range(4):
                q_all[zs * 4 + j, g * BLOCK : (g + 1) * BLOCK, :] = piece[
                    :, g * HEAD_DIM : (g + 1) * HEAD_DIM
                ]
            put_kv((zs * 2 + h) * 4 + j, piece[:, GQ:])
            put_kv((zs * 2 + 1 - h) * 4 + j, other[j][k])

    factor = math.log2(math.e) / math.sqrt(HEAD_DIM)
    keys = TILE * BLOCK
    lanes = 4 // CHAINS * BLOCK
    key_row = lax.broadcasted_iota(jnp.int32, (BLOCK, lanes), 0)
    query_row = lax.broadcasted_iota(jnp.int32, (BLOCK, lanes), 1) % BLOCK
    causal = key_row <= query_row

    for k in range(4):
        zd = (z + k) % 4

        def per_block(j, _, k=k, zd=zd):
            place = (zd * 2 + h) * 4 + j
            start = starts_ref[0, place]
            qs = [q_all[zd * 4 + j, i * lanes : (i + 1) * lanes, :] for i in range(CHAINS)]

            def tile(n, states, first):
                base = place - n * TILE
                kt = k_all[pl.ds(pl.multiple_of(base * BLOCK, BLOCK), keys), :]
                vt = jnp.concatenate([vt_all[base + u] for u in range(TILE)], axis=1)
                new = []
                for q, state in zip(qs, states):
                    s = lax.dot_general(
                        kt, q, (((1,), (1,)), ((), ())), preferred_element_type=jnp.float32
                    )
                    parts = []
                    for u in range(TILE):
                        part = s[u * BLOCK : (u + 1) * BLOCK]
                        if first and u == TILE - 1:
                            part = jnp.where(causal, part, NEG)
                        else:
                            part = jnp.where(base + u >= start + PAD, part, NEG)
                        parts.append(part)
                    s = jnp.concatenate(parts, axis=0)
                    peak = jnp.max(s, axis=0, keepdims=True)
                    if not first:
                        peak = jnp.maximum(peak, state[0])
                    w = jnp.exp2((s - peak) * factor)
                    w_sum = jnp.sum(w, axis=0, keepdims=True)
                    mixed = jnp.dot(vt, w.astype(jnp.bfloat16), preferred_element_type=jnp.float32)
                    if first:
                        new.append((peak, w_sum, mixed))
                    else:
                        keep = jnp.exp2((state[0] - peak) * factor)
                        new.append((peak, state[1] * keep + w_sum, state[2] * keep + mixed))
                return tuple(new)

            states = tile(0, (None,) * CHAINS, True)
            count = (place - start) // TILE + 1
            states = lax.fori_loop(1, count, lambda n, st: tile(n, st, False), states)
            rows = pl.ds(pl.multiple_of(j * BLOCK, BLOCK), BLOCK)
            for i, (_, total, acc) in enumerate(states):
                done = acc / total
                for g in range(4 // CHAINS):
                    cols = (4 // CHAINS * i + g) * HEAD_DIM
                    outs[k][rows, cols : cols + HEAD_DIM] = done[
                        :, g * BLOCK : (g + 1) * BLOCK
                    ].T.astype(jnp.bfloat16)
            return 0

        lax.fori_loop(0, 4, per_block, 0)


def attend(where, starts, blocks, pieces, other):
    vmem = pl.BlockSpec(memory_space=pltpu.VMEM)
    smem = pl.BlockSpec(memory_space=pltpu.SMEM)
    first = pl.BlockSpec((1, BLOCK, GW), lambda i: (0, 0, 0))
    return pl.pallas_call(
        attend_kernel,
        grid=(1,),
        out_shape=[jax.ShapeDtypeStruct((4 * BLOCK, GQ), jnp.bfloat16)] * 4,
        in_specs=[smem] * 2 + [first] * 4 + [vmem] * 16,
        out_specs=[vmem] * 4,
        scratch_shapes=[
            pltpu.VMEM((16, 4 * BLOCK, HEAD_DIM), jnp.bfloat16),
            pltpu.VMEM(((NB + PAD) * BLOCK, HEAD_DIM), jnp.bfloat16),
            pltpu.VMEM((NB + PAD, HEAD_DIM, BLOCK), jnp.bfloat16),
        ],
        name="attend",
    )(where, starts, *blocks, *pieces, *other)


def collect_kernel(*refs):
    out = refs[-1]
    out[0] = refs[0][0]
    for k in range(1, GROUPS):
        out[k] = refs[k][...]


def collect(block, came):
    first = pl.BlockSpec((1, BLOCK, GK), lambda i: (0, 0, GQ // GK))
    rest = pl.BlockSpec((BLOCK, GK), lambda i: (0, GQ // GK))
    return pl.pallas_call(
        collect_kernel,
        grid=(1,),
        out_shape=jax.ShapeDtypeStruct((GROUPS, BLOCK, GK), block.dtype),
        in_specs=[first] + [rest] * 3,
        out_specs=pl.BlockSpec((GROUPS, BLOCK, GK), lambda i: (0, 0, 0)),
        name="collect",
    )(block, *came)


def project_kernel(where_ref, *refs):
    parts, pieces, b_ref, out_ref = refs[:4], refs[4:9], refs[9], refs[10]
    rows, rows_b = refs[11:]
    y, core = where_ref[2], where_ref[3]
    step = pl.program_id(0)

    @pl.when(step == 0)
    def _():
        for k, part in enumerate(parts):
            group = (where_ref[0] + GROUPS - k) % GROUPS
            rows[:, pl.ds(pl.multiple_of(group * GQ, GQ), GQ)] = part[...]
        for n in range(16):
            head = n % 2 * 8 + n // 2
            rows_b[:, n * HEAD_DIM : (n + 1) * HEAD_DIM] = rows[
                :, head * HEAD_DIM : (head + 1) * HEAD_DIM
            ]

    @pl.when(step < COLS_A // WIDE)
    def _():
        far = (1 - y) * 1024
        firsts = (
            y * 1024,
            far + core * 512,
            far + core * 512 + 256,
            far + (1 - core) * 512,
            far + (1 - core) * 512 + 256,
        )
        total = None
        for first, piece in zip(firsts, pieces):
            depth = piece.shape[0]
            mine = rows[:, pl.ds(pl.multiple_of(first, 256), depth)]
            product = jnp.dot(mine, piece[...], preferred_element_type=jnp.float32)
            total = product if total is None else total + product
        out_ref[...] = total.astype(out_ref.dtype)

    @pl.when(step >= COLS_A // WIDE)
    def _():
        out_ref[...] = jnp.dot(
            rows_b[...], b_ref[...], preferred_element_type=jnp.float32
        ).astype(out_ref.dtype)


def project(where, parts, pieces, b):
    depth = b.shape[0]
    count = parts[0].shape[0]
    steps_a = COLS_A // WIDE
    part = pl.BlockSpec((count, GQ), lambda i, w: (0, 0))
    a_specs = [
        pl.BlockSpec((piece.shape[0], WIDE), lambda i, w: (0, jnp.minimum(i, steps_a - 1)))
        for piece in pieces
    ]
    b_spec = pl.BlockSpec((depth, WIDE), lambda i, w: (0, jnp.maximum(i - steps_a, 0)))
    cols = COLS_A + b.shape[1]
    return pl.pallas_call(
        project_kernel,
        out_shape=jax.ShapeDtypeStruct((count, cols), b.dtype),
        grid_spec=pltpu.PrefetchScalarGridSpec(
            num_scalar_prefetch=1,
            grid=(cols // WIDE,),
            in_specs=[part] * 4 + a_specs + [b_spec],
            out_specs=pl.BlockSpec((count, WIDE), lambda i, w: (0, i)),
            scratch_shapes=[pltpu.VMEM((count, depth), b.dtype)] * 2,
        ),
        name="project",
    )(where, *parts, *pieces, b)


def tie_kernel(where_ref, own_ref, far_ref, token_ref, out_ref):
    rows = own_ref.shape[0]
    y = where_ref[2]
    out_ref[pl.ds(pl.multiple_of(y * rows, rows), rows), :] = own_ref[...]
    out_ref[pl.ds(pl.multiple_of((1 - y) * rows, rows), rows), :] = far_ref[...]


def tie(where, own, far, token):
    rows, cols = own.shape
    half = pl.BlockSpec((rows, cols // 2), lambda i, w: (0, i))
    return pl.pallas_call(
        tie_kernel,
        out_shape=jax.ShapeDtypeStruct((2 * rows, cols), own.dtype),
        grid_spec=pltpu.PrefetchScalarGridSpec(
            num_scalar_prefetch=1,
            grid=(2,),
            in_specs=[half, half, pl.BlockSpec(memory_space=pl.ANY)],
            out_specs=pl.BlockSpec((2 * rows, cols // 2), lambda i, w: (0, i)),
        ),
        name="tie",
    )(where, own, far, token)


def y_shift(x, k):
    moves = []
    for dp in range(16):
        for seq in range(8):
            y = (seq % 2 * 2 + dp // 8 + k) % 4
            moves.append((dp * 8 + seq, (y % 2 * 8 + dp % 8) * 8 + seq // 2 * 2 + y // 2))
    return lax.ppermute(x, ("dp", "seq"), moves)


def body(queries, keys_values, doc_blocks, route_plan, out_weight):
    seq = lax.axis_index("seq")
    z, h = seq >> 1, seq & 1
    q, kv = queries[0], keys_values[0]
    qs = lax.ppermute(q, "dp", flip(1))
    kvs = lax.ppermute(kv, "dp", flip(1))
    dp = lax.axis_index("dp")
    core = dp & 1
    where = jnp.stack([z, h, dp >> 3, core]).astype(jnp.int32)
    own_a = lax.all_gather(
        out_weight[:, :COLS_A], "dp", axis=0, axis_index_groups=XC, tiled=True
    )
    far = lax.ppermute(out_weight[:, COLS_A:], "dp", flip(8))
    docs = doc_blocks[0]
    starts = jnp.sum((docs[None, :] < docs[:, None]).astype(jnp.int32), axis=1)[None]
    blocks = list(prep(where, route_plan, q, qs, kv, kvs))

    pieces, other = [], []
    for j in range(4):
        block = lax.switch(route_plan[0, j] >> 1, list(moves()), blocks[j])
        blocks[j] = block
        came = []
        for k in range(1, 4):
            came.append(z_shift(block[k], k))
        pieces += came
        mine = collect(block, came)
        other.append(lax.ppermute(mine, "seq", [(s, s ^ 1) for s in range(8)]))
    both = tie(where, out_weight[:, COLS_A:], far, blocks[3])
    weight_b = lax.all_gather(both, "dp", axis=0, axis_index_groups=XC, tiled=True)
    weight_a = [own_a]
    for n, shift in enumerate((-1, 1)):
        rows = lax.dynamic_slice_in_dim(own_a, core * 512 + n * 256, 256, 0)
        weight_a.append(y_shift(rows, shift))
    for n in range(2):
        weight_a.append(lax.ppermute(weight_a[1 + n], "dp", flip(1)))

    outs = attend(where, starts, blocks, pieces, other)
    parts = [outs[0]] + [z_shift(outs[k], k) for k in range(1, 4)]
    return project(where, parts, weight_a, weight_b)[None]


def solution(mesh):
    in_specs = (
        P("dp", "seq", None),
        P("dp", "seq", None),
        P("dp", None),
        P("seq", None),
        P("dp", None),
    )
    out_specs = P("dp", "seq", None)

    return jax.shard_map(body, mesh=mesh, in_specs=in_specs, out_specs=out_specs, check_vma=False)
```

```python
import math

import jax
import jax.numpy as jnp
from jax import lax
from jax.experimental import pallas as pl
from jax.experimental.pallas import tpu as pltpu
from jax.sharding import PartitionSpec as P

HEAD_DIM = 128
BLOCK = 128
GROUPS = 4
GQ = 512
GK = 256
GW = GQ + GK
TILE = 2
PAD = TILE - 1
CHAINS = 1
NB = 32
NEG = -1e30
XC = [list(range(8)), list(range(8, 16))]


def prep_kernel(z_ref, marks_ref, q_ref, qs_ref, k_ref, ks_ref, *out_refs):
    for j, out in enumerate(out_refs):
        rows = slice(j * BLOCK, (j + 1) * BLOCK)

        @pl.when(marks_ref[0, j] % 2 == 0)
        def _():
            out[0, :, :GQ] = q_ref[rows, :]
            out[0, :, GQ:] = k_ref[rows, :]

        @pl.when(marks_ref[0, j] % 2 != 0)
        def _():
            out[0, :, :GQ] = qs_ref[rows, :]
            out[0, :, GQ:] = ks_ref[rows, :]


def prep(z, marks, q, qs, kv, kvs):
    rows = q.shape[0]
    blocks = rows // BLOCK
    q_spec = pl.BlockSpec((rows, GQ), lambda k, z, m: (0, (z[0] + k) % GROUPS))
    k_spec = pl.BlockSpec((rows, GK), lambda k, z, m: (0, (z[0] + k) % GROUPS))
    o_spec = pl.BlockSpec((1, BLOCK, GW), lambda k, z, m: (k, 0, 0))
    return pl.pallas_call(
        prep_kernel,
        out_shape=[jax.ShapeDtypeStruct((GROUPS, BLOCK, GW), q.dtype)] * blocks,
        grid_spec=pltpu.PrefetchScalarGridSpec(
            num_scalar_prefetch=2,
            grid=(GROUPS,),
            in_specs=[q_spec, q_spec, k_spec, k_spec],
            out_specs=[o_spec] * blocks,
        ),
        name="prep",
    )(z, marks, q, qs, kv, kvs)


def flip(value):
    return [(i, i ^ value) for i in range(16)]


def moves():
    yield lambda x: x
    for code in range(1, 8):
        yield lambda x, code=code: lax.ppermute(x, "dp", flip(code << 1))


def z_shift(x, k):
    return lax.ppermute(x, "seq", [(s, (((s // 2) + k) % 4) * 2 + s % 2) for s in range(8)])


def attend_kernel(where_ref, starts_ref, *refs):
    own = [[refs[j]] + [refs[4 + 3 * j + k] for k in range(3)] for j in range(4)]
    other = refs[16:20]
    outs = refs[20:24]
    q_all, k_all, vt_all = refs[24:]
    z, h = where_ref[0], where_ref[1]

    k_all[pl.ds(0, PAD * BLOCK), :] = jnp.zeros((PAD * BLOCK, HEAD_DIM), k_all.dtype)
    vt_all[pl.ds(0, PAD)] = jnp.zeros((PAD, HEAD_DIM, BLOCK), vt_all.dtype)

    def put_kv(place, kv):
        k_all[pl.ds(pl.multiple_of((place + PAD) * BLOCK, BLOCK), BLOCK), :] = kv[:, :HEAD_DIM]
        vt_all[place + PAD] = kv[:, HEAD_DIM:].T

    for j in range(4):
        for k in range(4):
            zs = (z + 4 - k) % 4
            piece = own[j][k][0] if k == 0 else own[j][k][...]
            for g in range(4):
                q_all[zs * 4 + j, g * BLOCK : (g + 1) * BLOCK, :] = piece[
                    :, g * HEAD_DIM : (g + 1) * HEAD_DIM
                ]
            put_kv((zs * 2 + h) * 4 + j, piece[:, GQ:])
            put_kv((zs * 2 + 1 - h) * 4 + j, other[j][k])

    factor = math.log2(math.e) / math.sqrt(HEAD_DIM)
    keys = TILE * BLOCK
    lanes = 4 // CHAINS * BLOCK
    key_row = lax.broadcasted_iota(jnp.int32, (BLOCK, lanes), 0)
    query_row = lax.broadcasted_iota(jnp.int32, (BLOCK, lanes), 1) % BLOCK
    causal = key_row <= query_row

    for k in range(4):
        zd = (z + k) % 4

        def per_block(j, _, k=k, zd=zd):
            place = (zd * 2 + h) * 4 + j
            start = starts_ref[0, place]
            qs = [q_all[zd * 4 + j, i * lanes : (i + 1) * lanes, :] for i in range(CHAINS)]

            def tile(n, states, first):
                base = place - n * TILE
                kt = k_all[pl.ds(pl.multiple_of(base * BLOCK, BLOCK), keys), :]
                vt = jnp.concatenate([vt_all[base + u] for u in range(TILE)], axis=1)
                new = []
                for q, state in zip(qs, states):
                    s = lax.dot_general(
                        kt, q, (((1,), (1,)), ((), ())), preferred_element_type=jnp.float32
                    )
                    parts = []
                    for u in range(TILE):
                        part = s[u * BLOCK : (u + 1) * BLOCK]
                        if first and u == TILE - 1:
                            part = jnp.where(causal, part, NEG)
                        else:
                            part = jnp.where(base + u >= start + PAD, part, NEG)
                        parts.append(part)
                    s = jnp.concatenate(parts, axis=0)
                    peak = jnp.max(s, axis=0, keepdims=True)
                    if not first:
                        peak = jnp.maximum(peak, state[0])
                    w = jnp.exp2((s - peak) * factor)
                    w_sum = jnp.sum(w, axis=0, keepdims=True)
                    mixed = jnp.dot(vt, w.astype(jnp.bfloat16), preferred_element_type=jnp.float32)
                    if first:
                        new.append((peak, w_sum, mixed))
                    else:
                        keep = jnp.exp2((state[0] - peak) * factor)
                        new.append((peak, state[1] * keep + w_sum, state[2] * keep + mixed))
                return tuple(new)

            states = tile(0, (None,) * CHAINS, True)
            count = (place - start) // TILE + 1
            states = lax.fori_loop(1, count, lambda n, st: tile(n, st, False), states)
            rows = pl.ds(pl.multiple_of(j * BLOCK, BLOCK), BLOCK)
            for i, (_, total, acc) in enumerate(states):
                done = acc / total
                for g in range(4 // CHAINS):
                    cols = (4 // CHAINS * i + g) * HEAD_DIM
                    outs[k][rows, cols : cols + HEAD_DIM] = done[
                        :, g * BLOCK : (g + 1) * BLOCK
                    ].T.astype(jnp.bfloat16)
            return 0

        lax.fori_loop(0, 4, per_block, 0)


def attend(where, starts, blocks, pieces, other):
    vmem = pl.BlockSpec(memory_space=pltpu.VMEM)
    smem = pl.BlockSpec(memory_space=pltpu.SMEM)
    first = pl.BlockSpec((1, BLOCK, GW), lambda i: (0, 0, 0))
    return pl.pallas_call(
        attend_kernel,
        grid=(1,),
        out_shape=[jax.ShapeDtypeStruct((4 * BLOCK, GQ), jnp.bfloat16)] * 4,
        in_specs=[smem] * 2 + [first] * 4 + [vmem] * 16,
        out_specs=[vmem] * 4,
        scratch_shapes=[
            pltpu.VMEM((16, 4 * BLOCK, HEAD_DIM), jnp.bfloat16),
            pltpu.VMEM(((NB + PAD) * BLOCK, HEAD_DIM), jnp.bfloat16),
            pltpu.VMEM((NB + PAD, HEAD_DIM, BLOCK), jnp.bfloat16),
        ],
        name="attend",
    )(where, starts, *blocks, *pieces, *other)


def collect_kernel(*refs):
    out = refs[-1]
    out[0] = refs[0][0]
    for k in range(1, GROUPS):
        out[k] = refs[k][...]


def collect(block, came):
    first = pl.BlockSpec((1, BLOCK, GK), lambda i: (0, 0, GQ // GK))
    rest = pl.BlockSpec((BLOCK, GK), lambda i: (0, GQ // GK))
    return pl.pallas_call(
        collect_kernel,
        grid=(1,),
        out_shape=jax.ShapeDtypeStruct((GROUPS, BLOCK, GK), block.dtype),
        in_specs=[first] + [rest] * 3,
        out_specs=pl.BlockSpec((GROUPS, BLOCK, GK), lambda i: (0, 0, 0)),
        name="collect",
    )(block, *came)


def project_kernel(where_ref, *refs):
    parts, w_ref, out_ref, rows = refs[:4], refs[4], refs[5], refs[6]

    @pl.when(pl.program_id(0) == 0)
    def _():
        for k, part in enumerate(parts):
            group = (where_ref[0] + GROUPS - k) % GROUPS
            for g in range(GROUPS):
                head = group * GROUPS + g
                place = head % 8 * 2 + head // 8
                cols = pl.ds(pl.multiple_of(place * HEAD_DIM, HEAD_DIM), HEAD_DIM)
                rows[:, cols] = part[:, g * HEAD_DIM : (g + 1) * HEAD_DIM]

    out_ref[...] = jnp.dot(rows[...], w_ref[...], preferred_element_type=jnp.float32).astype(
        out_ref.dtype
    )


def project(where, parts, weight):
    depth, cols = weight.shape
    count = parts[0].shape[0]
    wide = 512
    part = pl.BlockSpec((count, GQ), lambda i, w: (0, 0))
    return pl.pallas_call(
        project_kernel,
        out_shape=jax.ShapeDtypeStruct((count, cols), weight.dtype),
        grid_spec=pltpu.PrefetchScalarGridSpec(
            num_scalar_prefetch=1,
            grid=(cols // wide,),
            in_specs=[part] * 4 + [pl.BlockSpec((depth, wide), lambda i, w: (0, i))],
            out_specs=pl.BlockSpec((count, wide), lambda i, w: (0, i)),
            scratch_shapes=[pltpu.VMEM((count, depth), weight.dtype)],
        ),
        name="project",
    )(where, *parts, weight)


def tie_kernel(where_ref, own_ref, lo_ref, hi_ref, token_ref, out_ref):
    rows = own_ref.shape[0]
    y = where_ref[2]
    far = pl.multiple_of((1 - y) * rows, rows)
    out_ref[pl.ds(pl.multiple_of(y * rows, rows), rows), :] = own_ref[...]
    out_ref[pl.ds(far, rows // 2), :] = lo_ref[...]
    out_ref[pl.ds(pl.multiple_of(far + rows // 2, rows // 2), rows // 2), :] = hi_ref[...]


def tie(where, own, lo, hi, token):
    rows, cols = own.shape
    half = pl.BlockSpec((rows // 2, cols // 4), lambda i, w: (0, i))
    return pl.pallas_call(
        tie_kernel,
        out_shape=jax.ShapeDtypeStruct((2 * rows, cols), own.dtype),
        grid_spec=pltpu.PrefetchScalarGridSpec(
            num_scalar_prefetch=1,
            grid=(4,),
            in_specs=[
                pl.BlockSpec((rows, cols // 4), lambda i, w: (0, i)),
                half,
                half,
                pl.BlockSpec(memory_space=pl.ANY),
            ],
            out_specs=pl.BlockSpec((2 * rows, cols // 4), lambda i, w: (0, i)),
        ),
        name="tie",
    )(where, own, lo, hi, token)


def y_shift(x, k):
    moves = []
    for dp in range(16):
        for seq in range(8):
            y = (seq % 2 * 2 + dp // 8 + k) % 4
            moves.append((dp * 8 + seq, (y % 2 * 8 + dp % 8) * 8 + seq // 2 * 2 + y // 2))
    return lax.ppermute(x, ("dp", "seq"), moves)


def body(queries, keys_values, doc_blocks, route_plan, out_weight):
    seq = lax.axis_index("seq")
    z, h = seq >> 1, seq & 1
    q, kv = queries[0], keys_values[0]
    qs = lax.ppermute(q, "dp", flip(1))
    kvs = lax.ppermute(kv, "dp", flip(1))
    where = jnp.stack([z, h, lax.axis_index("dp") >> 3]).astype(jnp.int32)
    far = []
    for n, shift in enumerate((1, -1)):
        rows = out_weight[n * 64 : (n + 1) * 64]
        far.append(y_shift(rows, shift))
    docs = doc_blocks[0]
    starts = jnp.sum((docs[None, :] < docs[:, None]).astype(jnp.int32), axis=1)[None]
    blocks = list(prep(where, route_plan, q, qs, kv, kvs))

    pieces, other = [], []
    for j in range(4):
        block = lax.switch(route_plan[0, j] >> 1, list(moves()), blocks[j])
        blocks[j] = block
        came = []
        for k in range(1, 4):
            came.append(z_shift(block[k], k))
        pieces += came
        mine = collect(block, came)
        other.append(lax.ppermute(mine, "seq", [(s, s ^ 1) for s in range(8)]))
    both = tie(where, out_weight, *far, blocks[3])
    weight = lax.all_gather(both, "dp", axis=0, axis_index_groups=XC, tiled=True)

    outs = attend(where, starts, blocks, pieces, other)
    parts = [outs[0]] + [z_shift(outs[k], k) for k in range(1, 4)]
    return project(where, parts, weight)[None]


def solution(mesh):
    in_specs = (
        P("dp", "seq", None),
        P("dp", "seq", None),
        P("dp", None),
        P("seq", None),
        P("dp", None),
    )
    out_specs = P("dp", "seq", None)

    return jax.shard_map(body, mesh=mesh, in_specs=in_specs, out_specs=out_specs, check_vma=False)
```

```python
import math

import jax
import jax.numpy as jnp
from jax import lax
from jax.experimental import pallas as pl
from jax.experimental.pallas import tpu as pltpu
from jax.sharding import PartitionSpec as P

HEAD_DIM = 128
BLOCK = 128
GROUPS = 4
GQ = 512
GK = 256
GW = GQ + GK
TILE = 2
PAD = TILE - 1
CHAINS = 1
NB = 32
NEG = -1e30
COLS_A = 2048
WIDE = 512
XC = [list(range(8)), list(range(8, 16))]


def prep_kernel(z_ref, marks_ref, q_ref, qs_ref, k_ref, ks_ref, *out_refs):
    for j, out in enumerate(out_refs):
        rows = slice(j * BLOCK, (j + 1) * BLOCK)

        @pl.when(marks_ref[0, j] % 2 == 0)
        def _():
            out[0, :, :GQ] = q_ref[rows, :]
            out[0, :, GQ:] = k_ref[rows, :]

        @pl.when(marks_ref[0, j] % 2 != 0)
        def _():
            out[0, :, :GQ] = qs_ref[rows, :]
            out[0, :, GQ:] = ks_ref[rows, :]


def prep(z, marks, q, qs, kv, kvs):
    rows = q.shape[0]
    blocks = rows // BLOCK
    q_spec = pl.BlockSpec((rows, GQ), lambda k, z, m: (0, (z[0] + k) % GROUPS))
    k_spec = pl.BlockSpec((rows, GK), lambda k, z, m: (0, (z[0] + k) % GROUPS))
    o_spec = pl.BlockSpec((1, BLOCK, GW), lambda k, z, m: (k, 0, 0))
    return pl.pallas_call(
        prep_kernel,
        out_shape=[jax.ShapeDtypeStruct((GROUPS, BLOCK, GW), q.dtype)] * blocks,
        grid_spec=pltpu.PrefetchScalarGridSpec(
            num_scalar_prefetch=2,
            grid=(GROUPS,),
            in_specs=[q_spec, q_spec, k_spec, k_spec],
            out_specs=[o_spec] * blocks,
        ),
        name="prep",
    )(z, marks, q, qs, kv, kvs)


def flip(value):
    return [(i, i ^ value) for i in range(16)]


def moves():
    yield lambda x: x
    for code in range(1, 8):
        yield lambda x, code=code: lax.ppermute(x, "dp", flip(code << 1))


def z_shift(x, k):
    return lax.ppermute(x, "seq", [(s, (((s // 2) + k) % 4) * 2 + s % 2) for s in range(8)])


def attend_kernel(where_ref, starts_ref, *refs):
    own = [[refs[j]] + [refs[4 + 3 * j + k] for k in range(3)] for j in range(4)]
    other = refs[16:20]
    outs = refs[20:24]
    q_all, k_all, vt_all = refs[24:]
    z, h = where_ref[0], where_ref[1]

    k_all[pl.ds(0, PAD * BLOCK), :] = jnp.zeros((PAD * BLOCK, HEAD_DIM), k_all.dtype)
    vt_all[pl.ds(0, PAD)] = jnp.zeros((PAD, HEAD_DIM, BLOCK), vt_all.dtype)

    def put_kv(place, kv):
        k_all[pl.ds(pl.multiple_of((place + PAD) * BLOCK, BLOCK), BLOCK), :] = kv[:, :HEAD_DIM]
        vt_all[place + PAD] = kv[:, HEAD_DIM:].T

    for j in range(4):
        for k in range(4):
            zs = (z + 4 - k) % 4
            piece = own[j][k][0] if k == 0 else own[j][k][...]
            for g in range(4):
                q_all[zs * 4 + j, g * BLOCK : (g + 1) * BLOCK, :] = piece[
                    :, g * HEAD_DIM : (g + 1) * HEAD_DIM
                ]
            put_kv((zs * 2 + h) * 4 + j, piece[:, GQ:])
            put_kv((zs * 2 + 1 - h) * 4 + j, other[j][k])

    factor = math.log2(math.e) / math.sqrt(HEAD_DIM)
    keys = TILE * BLOCK
    lanes = 4 // CHAINS * BLOCK
    key_row = lax.broadcasted_iota(jnp.int32, (BLOCK, lanes), 0)
    query_row = lax.broadcasted_iota(jnp.int32, (BLOCK, lanes), 1) % BLOCK
    causal = key_row <= query_row

    for k in range(4):
        zd = (z + k) % 4

        def per_block(j, _, k=k, zd=zd):
            place = (zd * 2 + h) * 4 + j
            start = starts_ref[0, place]
            qs = [q_all[zd * 4 + j, i * lanes : (i + 1) * lanes, :] for i in range(CHAINS)]

            def tile(n, states, first):
                base = place - n * TILE
                kt = k_all[pl.ds(pl.multiple_of(base * BLOCK, BLOCK), keys), :]
                vt = jnp.concatenate([vt_all[base + u] for u in range(TILE)], axis=1)
                new = []
                for q, state in zip(qs, states):
                    s = lax.dot_general(
                        kt, q, (((1,), (1,)), ((), ())), preferred_element_type=jnp.float32
                    )
                    parts = []
                    for u in range(TILE):
                        part = s[u * BLOCK : (u + 1) * BLOCK]
                        if first and u == TILE - 1:
                            part = jnp.where(causal, part, NEG)
                        else:
                            part = jnp.where(base + u >= start + PAD, part, NEG)
                        parts.append(part)
                    s = jnp.concatenate(parts, axis=0)
                    peak = jnp.max(s, axis=0, keepdims=True)
                    if not first:
                        peak = jnp.maximum(peak, state[0])
                    w = jnp.exp2((s - peak) * factor)
                    w_sum = jnp.sum(w, axis=0, keepdims=True)
                    mixed = jnp.dot(vt, w.astype(jnp.bfloat16), preferred_element_type=jnp.float32)
                    if first:
                        new.append((peak, w_sum, mixed))
                    else:
                        keep = jnp.exp2((state[0] - peak) * factor)
                        new.append((peak, state[1] * keep + w_sum, state[2] * keep + mixed))
                return tuple(new)

            states = tile(0, (None,) * CHAINS, True)
            count = (place - start) // TILE + 1
            states = lax.fori_loop(1, count, lambda n, st: tile(n, st, False), states)
            rows = pl.ds(pl.multiple_of(j * BLOCK, BLOCK), BLOCK)
            for i, (_, total, acc) in enumerate(states):
                done = acc / total
                for g in range(4 // CHAINS):
                    cols = (4 // CHAINS * i + g) * HEAD_DIM
                    outs[k][rows, cols : cols + HEAD_DIM] = done[
                        :, g * BLOCK : (g + 1) * BLOCK
                    ].T.astype(jnp.bfloat16)
            return 0

        lax.fori_loop(0, 4, per_block, 0)


def attend(where, starts, blocks, pieces, other):
    vmem = pl.BlockSpec(memory_space=pltpu.VMEM)
    smem = pl.BlockSpec(memory_space=pltpu.SMEM)
    first = pl.BlockSpec((1, BLOCK, GW), lambda i: (0, 0, 0))
    return pl.pallas_call(
        attend_kernel,
        grid=(1,),
        out_shape=[jax.ShapeDtypeStruct((4 * BLOCK, GQ), jnp.bfloat16)] * 4,
        in_specs=[smem] * 2 + [first] * 4 + [vmem] * 16,
        out_specs=[vmem] * 4,
        scratch_shapes=[
            pltpu.VMEM((16, 4 * BLOCK, HEAD_DIM), jnp.bfloat16),
            pltpu.VMEM(((NB + PAD) * BLOCK, HEAD_DIM), jnp.bfloat16),
            pltpu.VMEM((NB + PAD, HEAD_DIM, BLOCK), jnp.bfloat16),
        ],
        name="attend",
    )(where, starts, *blocks, *pieces, *other)


def collect_kernel(*refs):
    out = refs[-1]
    out[0] = refs[0][0]
    for k in range(1, GROUPS):
        out[k] = refs[k][...]


def collect(block, came):
    first = pl.BlockSpec((1, BLOCK, GK), lambda i: (0, 0, GQ // GK))
    rest = pl.BlockSpec((BLOCK, GK), lambda i: (0, GQ // GK))
    return pl.pallas_call(
        collect_kernel,
        grid=(1,),
        out_shape=jax.ShapeDtypeStruct((GROUPS, BLOCK, GK), block.dtype),
        in_specs=[first] + [rest] * 3,
        out_specs=pl.BlockSpec((GROUPS, BLOCK, GK), lambda i: (0, 0, 0)),
        name="collect",
    )(block, *came)


def project_kernel(where_ref, *refs):
    parts, pieces, b_ref, out_ref = refs[:4], refs[4:9], refs[9], refs[10]
    rows, rows_b = refs[11:]
    y, core = where_ref[2], where_ref[3]
    step = pl.program_id(0)

    @pl.when(step == 0)
    def _():
        for k, part in enumerate(parts):
            group = (where_ref[0] + GROUPS - k) % GROUPS
            rows[:, pl.ds(pl.multiple_of(group * GQ, GQ), GQ)] = part[...]
        for n in range(16):
            head = n % 2 * 8 + n // 2
            rows_b[:, n * HEAD_DIM : (n + 1) * HEAD_DIM] = rows[
                :, head * HEAD_DIM : (head + 1) * HEAD_DIM
            ]

    @pl.when(step < COLS_A // WIDE)
    def _():
        far = (1 - y) * 1024
        firsts = (
            y * 1024,
            far + core * 512,
            far + core * 512 + 256,
            far + (1 - core) * 512,
            far + (1 - core) * 512 + 256,
        )
        total = None
        for first, piece in zip(firsts, pieces):
            depth = piece.shape[0]
            mine = rows[:, pl.ds(pl.multiple_of(first, 256), depth)]
            product = jnp.dot(mine, piece[...], preferred_element_type=jnp.float32)
            total = product if total is None else total + product
        out_ref[...] = total.astype(out_ref.dtype)

    @pl.when(step >= COLS_A // WIDE)
    def _():
        out_ref[...] = jnp.dot(
            rows_b[...], b_ref[...], preferred_element_type=jnp.float32
        ).astype(out_ref.dtype)


def project(where, parts, pieces, b):
    depth = b.shape[0]
    count = parts[0].shape[0]
    steps_a = COLS_A // WIDE
    part = pl.BlockSpec((count, GQ), lambda i, w: (0, 0))
    a_specs = [
        pl.BlockSpec((piece.shape[0], WIDE), lambda i, w: (0, jnp.minimum(i, steps_a - 1)))
        for piece in pieces
    ]
    b_spec = pl.BlockSpec((depth, WIDE), lambda i, w: (0, jnp.maximum(i - steps_a, 0)))
    cols = COLS_A + b.shape[1]
    return pl.pallas_call(
        project_kernel,
        out_shape=jax.ShapeDtypeStruct((count, cols), b.dtype),
        grid_spec=pltpu.PrefetchScalarGridSpec(
            num_scalar_prefetch=1,
            grid=(cols // WIDE,),
            in_specs=[part] * 4 + a_specs + [b_spec],
            out_specs=pl.BlockSpec((count, WIDE), lambda i, w: (0, i)),
            scratch_shapes=[pltpu.VMEM((count, depth), b.dtype)] * 2,
        ),
        name="project",
    )(where, *parts, *pieces, b)


def tie_kernel(where_ref, a_ref, b_ref, lo_ref, hi_ref, token_ref, one_ref, both_ref):
    rows = b_ref.shape[0]
    y = where_ref[2]
    far = pl.multiple_of((1 - y) * rows, rows)
    one_ref[...] = a_ref[...]
    both_ref[pl.ds(pl.multiple_of(y * rows, rows), rows), :] = b_ref[...]
    both_ref[pl.ds(far, rows // 2), :] = lo_ref[...]
    both_ref[pl.ds(pl.multiple_of(far + rows // 2, rows // 2), rows // 2), :] = hi_ref[...]


def tie(where, own, lo, hi, token):
    rows, cols = own.shape
    half = cols // 2
    wide = half // 2
    thin = pl.BlockSpec((rows // 2, wide), lambda i, w: (0, i))
    one = pl.BlockSpec((rows, wide), lambda i, w: (0, i))
    return pl.pallas_call(
        tie_kernel,
        out_shape=[
            jax.ShapeDtypeStruct((rows, half), own.dtype),
            jax.ShapeDtypeStruct((2 * rows, half), own.dtype),
        ],
        grid_spec=pltpu.PrefetchScalarGridSpec(
            num_scalar_prefetch=1,
            grid=(2,),
            in_specs=[
                one,
                pl.BlockSpec((rows, wide), lambda i, w: (0, i + 2)),
                thin,
                thin,
                pl.BlockSpec(memory_space=pl.ANY),
            ],
            out_specs=[one, pl.BlockSpec((2 * rows, wide), lambda i, w: (0, i))],
        ),
        name="tie",
    )(where, own, own, lo, hi, token)


def y_shift(x, k):
    moves = []
    for dp in range(16):
        for seq in range(8):
            y = (seq % 2 * 2 + dp // 8 + k) % 4
            moves.append((dp * 8 + seq, (y % 2 * 8 + dp % 8) * 8 + seq // 2 * 2 + y // 2))
    return lax.ppermute(x, ("dp", "seq"), moves)


def body(queries, keys_values, doc_blocks, route_plan, out_weight):
    seq = lax.axis_index("seq")
    z, h = seq >> 1, seq & 1
    q, kv = queries[0], keys_values[0]
    qs = lax.ppermute(q, "dp", flip(1))
    kvs = lax.ppermute(kv, "dp", flip(1))
    dp = lax.axis_index("dp")
    core = dp & 1
    where = jnp.stack([z, h, dp >> 3, core]).astype(jnp.int32)
    far = []
    for n, shift in enumerate((1, -1)):
        rows = out_weight[n * 64 : (n + 1) * 64, COLS_A:]
        far.append(y_shift(rows, shift))
    docs = doc_blocks[0]
    starts = jnp.sum((docs[None, :] < docs[:, None]).astype(jnp.int32), axis=1)[None]
    blocks = list(prep(where, route_plan, q, qs, kv, kvs))

    pieces, other = [], []
    for j in range(4):
        block = lax.switch(route_plan[0, j] >> 1, list(moves()), blocks[j])
        blocks[j] = block
        came = []
        for k in range(1, 4):
            came.append(z_shift(block[k], k))
        pieces += came
        mine = collect(block, came)
        other.append(lax.ppermute(mine, "seq", [(s, s ^ 1) for s in range(8)]))
    one, both = tie(where, out_weight, *far, blocks[3])
    own_a = lax.all_gather(one, "dp", axis=0, axis_index_groups=XC, tiled=True)
    weight_b = lax.all_gather(both, "dp", axis=0, axis_index_groups=XC, tiled=True)
    weight_a = [own_a]
    for n, shift in enumerate((-1, 1)):
        rows = lax.dynamic_slice_in_dim(own_a, core * 512 + n * 256, 256, 0)
        weight_a.append(y_shift(rows, shift))
    for n in range(2):
        weight_a.append(lax.ppermute(weight_a[1 + n], "dp", flip(1)))

    outs = attend(where, starts, blocks, pieces, other)
    parts = [outs[0]]
    for k in range(1, 4):
        parts.append(z_shift(outs[k], k))
    return project(where, parts, weight_a, weight_b)[None]


def solution(mesh):
    in_specs = (
        P("dp", "seq", None),
        P("dp", "seq", None),
        P("dp", None),
        P("seq", None),
        P("dp", None),
    )
    out_specs = P("dp", "seq", None)

    return jax.shard_map(body, mesh=mesh, in_specs=in_specs, out_specs=out_specs, check_vma=False)
```

```python
import math

import jax
import jax.numpy as jnp
from jax import lax
from jax.experimental import pallas as pl
from jax.experimental.pallas import tpu as pltpu
from jax.sharding import PartitionSpec as P

HEAD_DIM = 128
BLOCK = 128
GROUPS = 4
GQ = 512
GK = 256
GW = GQ + GK
TILE = 2
PAD = TILE - 1
CHAINS = 1
NB = 32
NEG = -1e30
XC = [list(range(8)), list(range(8, 16))]


def prep_kernel(z_ref, marks_ref, q_ref, qs_ref, k_ref, ks_ref, *out_refs):
    for j, out in enumerate(out_refs):
        rows = slice(j * BLOCK, (j + 1) * BLOCK)

        @pl.when(marks_ref[0, j] % 2 == 0)
        def _():
            out[0, :, :GQ] = q_ref[rows, :]
            out[0, :, GQ:] = k_ref[rows, :]

        @pl.when(marks_ref[0, j] % 2 != 0)
        def _():
            out[0, :, :GQ] = qs_ref[rows, :]
            out[0, :, GQ:] = ks_ref[rows, :]


def prep(z, marks, q, qs, kv, kvs):
    rows = q.shape[0]
    blocks = rows // BLOCK
    q_spec = pl.BlockSpec((rows, GQ), lambda k, z, m: (0, (z[0] + k) % GROUPS))
    k_spec = pl.BlockSpec((rows, GK), lambda k, z, m: (0, (z[0] + k) % GROUPS))
    o_spec = pl.BlockSpec((1, BLOCK, GW), lambda k, z, m: (k, 0, 0))
    return pl.pallas_call(
        prep_kernel,
        out_shape=[jax.ShapeDtypeStruct((GROUPS, BLOCK, GW), q.dtype)] * blocks,
        grid_spec=pltpu.PrefetchScalarGridSpec(
            num_scalar_prefetch=2,
            grid=(GROUPS,),
            in_specs=[q_spec, q_spec, k_spec, k_spec],
            out_specs=[o_spec] * blocks,
        ),
        name="prep",
    )(z, marks, q, qs, kv, kvs)


def flip(value):
    return [(i, i ^ value) for i in range(16)]


def moves():
    yield lambda x: x
    for code in range(1, 8):
        yield lambda x, code=code: lax.ppermute(x, "dp", flip(code << 1))


def z_shift(x, k):
    return lax.ppermute(x, "seq", [(s, (((s // 2) + k) % 4) * 2 + s % 2) for s in range(8)])


def attend_kernel(where_ref, starts_ref, *refs):
    own = [[refs[j]] + [refs[4 + 3 * j + k] for k in range(3)] for j in range(4)]
    other = refs[16:20]
    outs = refs[20:24]
    q_all, k_all, vt_all = refs[24:]
    z, h = where_ref[0], where_ref[1]

    k_all[pl.ds(0, PAD * BLOCK), :] = jnp.zeros((PAD * BLOCK, HEAD_DIM), k_all.dtype)
    vt_all[pl.ds(0, PAD)] = jnp.zeros((PAD, HEAD_DIM, BLOCK), vt_all.dtype)

    def put_kv(place, kv):
        k_all[pl.ds(pl.multiple_of((place + PAD) * BLOCK, BLOCK), BLOCK), :] = kv[:, :HEAD_DIM]
        vt_all[place + PAD] = kv[:, HEAD_DIM:].T

    for j in range(4):
        for k in range(4):
            zs = (z + 4 - k) % 4
            piece = own[j][k][0] if k == 0 else own[j][k][...]
            for g in range(4):
                q_all[zs * 4 + j, g * BLOCK : (g + 1) * BLOCK, :] = piece[
                    :, g * HEAD_DIM : (g + 1) * HEAD_DIM
                ]
            put_kv((zs * 2 + h) * 4 + j, piece[:, GQ:])
            put_kv((zs * 2 + 1 - h) * 4 + j, other[j][k])

    factor = math.log2(math.e) / math.sqrt(HEAD_DIM)
    keys = TILE * BLOCK
    lanes = 4 // CHAINS * BLOCK
    key_row = lax.broadcasted_iota(jnp.int32, (BLOCK, lanes), 0)
    query_row = lax.broadcasted_iota(jnp.int32, (BLOCK, lanes), 1) % BLOCK
    causal = key_row <= query_row

    for k in range(4):
        zd = (z + k) % 4

        def per_block(j, _, k=k, zd=zd):
            place = (zd * 2 + h) * 4 + j
            start = starts_ref[0, place]
            qs = [q_all[zd * 4 + j, i * lanes : (i + 1) * lanes, :] for i in range(CHAINS)]

            def tile(n, states, first):
                base = place - n * TILE
                kt = k_all[pl.ds(pl.multiple_of(base * BLOCK, BLOCK), keys), :]
                vt = jnp.concatenate([vt_all[base + u] for u in range(TILE)], axis=1)
                new = []
                for q, state in zip(qs, states):
                    s = lax.dot_general(
                        kt, q, (((1,), (1,)), ((), ())), preferred_element_type=jnp.float32
                    )
                    parts = []
                    for u in range(TILE):
                        part = s[u * BLOCK : (u + 1) * BLOCK]
                        if first and u == TILE - 1:
                            part = jnp.where(causal, part, NEG)
                        else:
                            part = jnp.where(base + u >= start + PAD, part, NEG)
                        parts.append(part)
                    s = jnp.concatenate(parts, axis=0)
                    peak = jnp.max(s, axis=0, keepdims=True)
                    if not first:
                        peak = jnp.maximum(peak, state[0])
                    w = jnp.exp2((s - peak) * factor)
                    w_sum = jnp.sum(w, axis=0, keepdims=True)
                    mixed = jnp.dot(vt, w.astype(jnp.bfloat16), preferred_element_type=jnp.float32)
                    if first:
                        new.append((peak, w_sum, mixed))
                    else:
                        keep = jnp.exp2((state[0] - peak) * factor)
                        new.append((peak, state[1] * keep + w_sum, state[2] * keep + mixed))
                return tuple(new)

            states = tile(0, (None,) * CHAINS, True)
            count = (place - start) // TILE + 1
            states = lax.fori_loop(1, count, lambda n, st: tile(n, st, False), states)
            rows = pl.ds(pl.multiple_of(j * BLOCK, BLOCK), BLOCK)
            for i, (_, total, acc) in enumerate(states):
                done = acc / total
                for g in range(4 // CHAINS):
                    cols = (4 // CHAINS * i + g) * HEAD_DIM
                    outs[k][rows, cols : cols + HEAD_DIM] = done[
                        :, g * BLOCK : (g + 1) * BLOCK
                    ].T.astype(jnp.bfloat16)
            return 0

        lax.fori_loop(0, 4, per_block, 0)


def attend(where, starts, blocks, pieces, other):
    vmem = pl.BlockSpec(memory_space=pltpu.VMEM)
    smem = pl.BlockSpec(memory_space=pltpu.SMEM)
    first = pl.BlockSpec((1, BLOCK, GW), lambda i: (0, 0, 0))
    return pl.pallas_call(
        attend_kernel,
        grid=(1,),
        out_shape=[jax.ShapeDtypeStruct((4 * BLOCK, GQ), jnp.bfloat16)] * 4,
        in_specs=[smem] * 2 + [first] * 4 + [vmem] * 16,
        out_specs=[vmem] * 4,
        scratch_shapes=[
            pltpu.VMEM((16, 4 * BLOCK, HEAD_DIM), jnp.bfloat16),
            pltpu.VMEM(((NB + PAD) * BLOCK, HEAD_DIM), jnp.bfloat16),
            pltpu.VMEM((NB + PAD, HEAD_DIM, BLOCK), jnp.bfloat16),
        ],
        name="attend",
    )(where, starts, *blocks, *pieces, *other)


def collect_kernel(*refs):
    out = refs[-1]
    out[0] = refs[0][0]
    for k in range(1, GROUPS):
        out[k] = refs[k][...]


def collect(block, came):
    first = pl.BlockSpec((1, BLOCK, GK), lambda i: (0, 0, GQ // GK))
    rest = pl.BlockSpec((BLOCK, GK), lambda i: (0, GQ // GK))
    return pl.pallas_call(
        collect_kernel,
        grid=(1,),
        out_shape=jax.ShapeDtypeStruct((GROUPS, BLOCK, GK), block.dtype),
        in_specs=[first] + [rest] * 3,
        out_specs=pl.BlockSpec((GROUPS, BLOCK, GK), lambda i: (0, 0, 0)),
        name="collect",
    )(block, *came)


def project_kernel(where_ref, *refs):
    parts, w_ref, out_ref, rows = refs[:4], refs[4], refs[5], refs[6]

    @pl.when(pl.program_id(0) == 0)
    def _():
        for k, part in enumerate(parts):
            group = (where_ref[0] + GROUPS - k) % GROUPS
            for g in range(GROUPS):
                head = group * GROUPS + g
                place = head % 8 * 2 + head // 8
                cols = pl.ds(pl.multiple_of(place * HEAD_DIM, HEAD_DIM), HEAD_DIM)
                rows[:, cols] = part[:, g * HEAD_DIM : (g + 1) * HEAD_DIM]

    out_ref[...] = jnp.dot(rows[...], w_ref[...], preferred_element_type=jnp.float32).astype(
        out_ref.dtype
    )


def project(where, parts, weight):
    depth, cols = weight.shape
    count = parts[0].shape[0]
    wide = 512
    part = pl.BlockSpec((count, GQ), lambda i, w: (0, 0))
    return pl.pallas_call(
        project_kernel,
        out_shape=jax.ShapeDtypeStruct((count, cols), weight.dtype),
        grid_spec=pltpu.PrefetchScalarGridSpec(
            num_scalar_prefetch=1,
            grid=(cols // wide,),
            in_specs=[part] * 4 + [pl.BlockSpec((depth, wide), lambda i, w: (0, i))],
            out_specs=pl.BlockSpec((count, wide), lambda i, w: (0, i)),
            scratch_shapes=[pltpu.VMEM((count, depth), weight.dtype)],
        ),
        name="project",
    )(where, *parts, weight)


def tie_kernel(where_ref, own_ref, lo_ref, hi_ref, token_ref, out_ref):
    rows = own_ref.shape[0]
    y = where_ref[2]
    far = pl.multiple_of((1 - y) * rows, rows)
    out_ref[pl.ds(pl.multiple_of(y * rows, rows), rows), :] = own_ref[...]
    out_ref[pl.ds(far, rows // 2), :] = lo_ref[...]
    out_ref[pl.ds(pl.multiple_of(far + rows // 2, rows // 2), rows // 2), :] = hi_ref[...]


def tie(where, own, lo, hi, token):
    rows, cols = own.shape
    half = pl.BlockSpec((rows // 2, cols // 2), lambda i, w: (0, i))
    return pl.pallas_call(
        tie_kernel,
        out_shape=jax.ShapeDtypeStruct((2 * rows, cols), own.dtype),
        grid_spec=pltpu.PrefetchScalarGridSpec(
            num_scalar_prefetch=1,
            grid=(2,),
            in_specs=[
                pl.BlockSpec((rows, cols // 2), lambda i, w: (0, i)),
                half,
                half,
                pl.BlockSpec(memory_space=pl.ANY),
            ],
            out_specs=pl.BlockSpec((2 * rows, cols // 2), lambda i, w: (0, i)),
        ),
        name="tie",
    )(where, own, lo, hi, token)


def y_shift(x, k):
    moves = []
    for dp in range(16):
        for seq in range(8):
            y = (seq % 2 * 2 + dp // 8 + k) % 4
            moves.append((dp * 8 + seq, (y % 2 * 8 + dp % 8) * 8 + seq // 2 * 2 + y // 2))
    return lax.ppermute(x, ("dp", "seq"), moves)


def body(queries, keys_values, doc_blocks, route_plan, out_weight):
    seq = lax.axis_index("seq")
    z, h = seq >> 1, seq & 1
    q, kv = queries[0], keys_values[0]
    qs = lax.ppermute(q, "dp", flip(1))
    kvs = lax.ppermute(kv, "dp", flip(1))
    where = jnp.stack([z, h, lax.axis_index("dp") >> 3]).astype(jnp.int32)
    far = []
    for n, shift in enumerate((1, -1)):
        rows = out_weight[n * 64 : (n + 1) * 64]
        far.append(y_shift(rows, shift))
    docs = doc_blocks[0]
    starts = jnp.sum((docs[None, :] < docs[:, None]).astype(jnp.int32), axis=1)[None]
    blocks = list(prep(where, route_plan, q, qs, kv, kvs))

    pieces, other = [], []
    for j in range(4):
        block = lax.switch(route_plan[0, j] >> 1, list(moves()), blocks[j])
        blocks[j] = block
        came = []
        for k in range(1, 4):
            came.append(z_shift(block[k], k))
        pieces += came
        mine = collect(block, came)
        other.append(lax.ppermute(mine, "seq", [(s, s ^ 1) for s in range(8)]))
    both = tie(where, out_weight, *far, blocks[3])
    weight = lax.all_gather(both, "dp", axis=0, axis_index_groups=XC, tiled=True)

    outs = attend(where, starts, blocks, pieces, other)
    parts = [outs[0]] + [z_shift(outs[k], k) for k in range(1, 4)]
    return project(where, parts, weight)[None]


def solution(mesh):
    in_specs = (
        P("dp", "seq", None),
        P("dp", "seq", None),
        P("dp", None),
        P("seq", None),
        P("dp", None),
    )
    out_specs = P("dp", "seq", None)

    return jax.shard_map(body, mesh=mesh, in_specs=in_specs, out_specs=out_specs, check_vma=False)
```
